32 devices in a mesh: ctx: 16 (over z, y, x), fsdp: 2 (over core).
Axes of the slice: x: 2, y: 2, z: 4, core: 2. Of those that a mesh axis runs over, the one named last changes fastest.
Arguments:
- xbc: bfloat16 [4096, 9216], P(('fsdp', 'ctx')), may hold values from -6 to 6
- dt: bfloat16 [4096, 128], P(('fsdp', 'ctx')), may hold values from -5 to 5
- conv_weight: float32 [4, 9216], P(None, 'fsdp'), may hold values from -3 to 3
- conv_bias: float32 [9216], P('fsdp'), may hold values from -0.5 to 0.5
- dt_bias: float32 [128], P('fsdp'), may hold values from -1 to 1
- a_log: float32 [128], P('fsdp'), may hold values from -14 to -3
- skip: float32 [128], P('fsdp'), may hold values from 0.5 to 2
- norm_gain: float32 [8192], P('fsdp'), may hold values from 0.5 to 1.5
Outputs:
- mixed: bfloat16 [4096, 8192], P(('fsdp', 'ctx'))
The draws below stay inside these ranges and needn't reach their ends.
All inputs are finite; a program needn't handle non-finite values.
Results may differ from the reference program's by a relative error of at most 0.0051.
Values may be sent and summed in bfloat16 or wider, within the bound.
A program may use at most 128 MiB of HBM per device.

```python
import jax
import jax.numpy as jnp
from jax import lax

HEADS = 128
P_SIZE = 64
N = 128
GROUPS = 4
DI = 8192
CH = 9216
LENGTH = 4096


def draw_a_log(key, part):
    pick_key, slow_key, fast_key = jax.random.split(jax.random.fold_in(key, 11), 3)
    share = 0.5
    fast_heads = jax.random.bernoulli(pick_key, share, (HEADS,))
    slow_rate = jnp.log(0.1 / LENGTH) + jax.random.uniform(slow_key, (HEADS,), jnp.float32) * jnp.log(15.0)
    fast_rate = jnp.log(0.015) + jax.random.uniform(fast_key, (HEADS,), jnp.float32) * jnp.log(3.0)
    return jnp.where(fast_heads, fast_rate, slow_rate).astype(jnp.float32)


def shard_levels(rng, extent, cuts, low, largest):
    level = 1.0
    for dim, shards_of in cuts:
        steps = jax.random.uniform(jax.random.fold_in(jax.random.fold_in(rng, 6), dim), (shards_of,), jnp.float32, low / len(cuts), largest / len(cuts))
        level = level * jnp.repeat(jnp.exp(steps), extent[dim] // shards_of).reshape((-1,) + (1,) * (len(extent) - 1 - dim))
    return level


def normal_values(key, shape, scale, reach, cuts=(), kind=jnp.bfloat16):
    values = jax.random.normal(key, shape, jnp.float32) * scale
    if len(cuts) > 0:
        values = shard_levels(key, shape, cuts, -0.22, 0.18) * values
    return jnp.clip(values, min=-reach, max=reach).astype(kind)


def setup_inputs(seed: int = 0) -> dict:
    key_of = jax.random.split(jax.random.key(seed), 9)
    return {
        "xbc": normal_values(key_of[0], (LENGTH, CH), 1.0, 6.0, ((0, 32),)),
        "dt": normal_values(key_of[1], (LENGTH, HEADS), 1.0, 5.0, ((0, 32),)),
        "conv_weight": normal_values(key_of[2], (4, CH), 4 ** -0.5, 3.0, ((1, 2),), jnp.float32),
        "conv_bias": jnp.clip(jax.random.uniform(key_of[3], (CH,), jnp.float32, -0.5, 0.5) * shard_levels(key_of[3], (CH,), ((0, 2),), -0.4, 0.0), -0.5, 0.5),
        "dt_bias": jnp.clip(jax.random.uniform(key_of[4], (HEADS,), jnp.float32, -1.0, 1.0) * shard_levels(key_of[4], (HEADS,), ((0, 2),), -0.4, 0.0), -1.0, 1.0),
        "a_log": draw_a_log(jax.random.fold_in(key_of[8], 71), 0),
        "skip": jnp.clip(0.5 + 1.5 * jax.random.uniform(key_of[6], (HEADS,), jnp.float32) ** shard_levels(key_of[6], (HEADS,), ((0, 2),), -0.2, 0.2), 0.5, 2.0),
        "norm_gain": jnp.clip(1.0 + 0.1 * jax.random.normal(key_of[7], (DI,), jnp.float32), 0.5, 1.5),
    }


PRECISE = lax.Precision.HIGHEST

def conv_silu(extended, taps, offsets):
    row_count = extended.shape[0] - 3
    total = offsets[None, :] + taps[0][None, :] * extended[0:row_count].astype(jnp.float32)
    for kernel_tap in range(1, 4):
        total = total + taps[kernel_tap][None, :] * extended[kernel_tap:kernel_tap + row_count].astype(jnp.float32)
    return jax.nn.silu(total).astype(jnp.bfloat16)

def span_terms(values, keys_in, queries, delta, decay, state):
    values_f = values.astype(jnp.float32)
    keys_f = keys_in.astype(jnp.float32)
    queries_f = queries.astype(jnp.float32)
    block_rows = values.shape[0]
    cumulative = jnp.cumsum(decay, axis=0)
    lower = (lax.broadcasted_iota(jnp.int32, (block_rows, block_rows), 0) >= lax.broadcasted_iota(jnp.int32, (block_rows, block_rows), 1))[:, :, None, None]
    spread = cumulative[:, None] - cumulative[None, :]
    segment = jnp.where(lower, jnp.exp(jnp.where(lower, spread, 0.0)), 0.0)
    scores = jnp.einsum('tgn,sgn->tsg', queries_f, keys_f, precision=PRECISE)
    weights = segment * scores[..., None] * delta[None]
    inner = jnp.einsum('tsgk,sgkp->tgkp', weights, values_f, precision=PRECISE)
    carried = jnp.exp(cumulative)[..., None] * jnp.einsum('tgn,gkpn->tgkp', queries_f, state, precision=PRECISE)
    tail_weight = jnp.exp(cumulative[-1][None] - cumulative) * delta
    updated = jnp.exp(cumulative[-1])[..., None, None] * state + jnp.einsum('sgk,sgn,sgkp->gkpn', tail_weight, keys_f, values_f, precision=PRECISE)
    return (inner + carried, updated)

def span_sweep(values, keys_in, queries, delta, decay, state, block_rows):
    blocks = values.shape[0] // block_rows

    def split_rows(array):
        return array.reshape((blocks, block_rows) + array.shape[1:])

    def advance(carry, pieces):
        result, updated = span_terms(pieces[0], pieces[1], pieces[2], pieces[3], pieces[4], carry)
        return (updated, result)
    last_state, results = lax.scan(advance, state, (split_rows(values), split_rows(keys_in), split_rows(queries), split_rows(delta), split_rows(decay)))
    return (results.reshape(values.shape), last_state)

def group_norm(mixed_in, gain):
    row_count = mixed_in.shape[0]
    values = mixed_in.astype(jnp.float32).reshape(row_count, GROUPS, -1)
    meansq = lax.optimization_barrier(jnp.mean(values * values, axis=-1, keepdims=True))
    scaled = values * lax.rsqrt(meansq + 1e-05) * gain.reshape(1, GROUPS, -1)
    return scaled.reshape(row_count, -1).astype(jnp.bfloat16)

def one_sequence(token_rows, rates, conv_weight, conv_bias, dt_bias, a_log, skip, norm_gain):
    length = token_rows.shape[0]
    inner_width = HEADS * P_SIZE
    per_group = HEADS // GROUPS
    padded = jnp.concatenate([jnp.zeros((3, token_rows.shape[1]), jnp.bfloat16), token_rows], axis=0)
    conv_out = conv_silu(padded, conv_weight, conv_bias)
    values = conv_out[:, :inner_width].reshape(length, GROUPS, per_group, P_SIZE)
    keys_in = conv_out[:, inner_width:inner_width + GROUPS * N].reshape(length, GROUPS, N)
    queries = conv_out[:, inner_width + GROUPS * N:].reshape(length, GROUPS, N)
    delta = jax.nn.softplus(rates.astype(jnp.float32) + dt_bias[None, :]).reshape(length, GROUPS, per_group)
    decay = -jnp.exp(a_log).reshape(1, GROUPS, per_group) * delta
    state = jnp.zeros((GROUPS, per_group, P_SIZE, N), jnp.float32)
    swept = span_sweep(values, keys_in, queries, delta, decay, state, min(64, length))
    outputs = swept[0] + skip.reshape(1, GROUPS, per_group, 1) * values.astype(jnp.float32)
    return group_norm(outputs.reshape(length, inner_width).astype(jnp.bfloat16), norm_gain)

def reference(xbc, dt, conv_weight, conv_bias, dt_bias, a_log, skip, norm_gain):
    return one_sequence(xbc, dt, conv_weight, conv_bias, dt_bias, a_log, skip, norm_gain)
```

```python
import jax
import jax.numpy as jnp
from jax import lax
from jax.experimental import pallas as pl
from jax.experimental.pallas import tpu as pltpu
from jax.sharding import PartitionSpec as P

P_SIZE = 64
N = 128
GROUPS = 4
HALO = 16
WIDTH = 256
F32, BF16 = jnp.float32, jnp.bfloat16
HBM = pl.BlockSpec(memory_space=pltpu.HBM)
WHOLE = pl.BlockSpec(memory_space=pltpu.VMEM)


def place():
    f, c = lax.axis_index("fsdp"), lax.axis_index("ctx")
    nz = lax.axis_size("ctx") // GROUPS
    nf = lax.axis_size("fsdp")
    g, z = lax.rem(c, GROUPS), c // GROUPS
    return f, c, g, z, nz, nf, f * nz + z


def device(seg, g, nz):
    return {"fsdp": seg // nz, "ctx": lax.rem(seg, nz) * GROUPS + g}


def lanes(index, size):
    return pl.ds(pl.multiple_of(index * size, 128), size)


def hi_lo(v):
    hi = v.astype(BF16)
    return jnp.concatenate([hi, (v - hi.astype(F32)).astype(BF16)], axis=1)


def dot(a, b, dims=((1,), (0,))):
    return lax.dot_general(a, b, (dims, ((), ())), preferred_element_type=F32)


def fill_selection(sel, g):
    heads, width = sel.shape[0] // 2, sel.shape[1]
    per_group = width // P_SIZE
    row = lax.broadcasted_iota(jnp.int32, sel.shape, 0)
    col = lax.broadcasted_iota(jnp.int32, sel.shape, 1)
    row = jnp.where(row >= heads, row - heads, row)
    sel[...] = jnp.where(row == g * per_group + col // P_SIZE, 1.0, 0.0).astype(BF16)


def silu_conv(ext, start, taps, bias, at, size):
    rows = ext.shape[0] - 8
    total = bias
    for k in range(4):
        total = total + taps[k : k + 1, at] * ext[5 + k : 5 + k + rows, start : start + size]
    return (total / (1.0 + jnp.exp(-total))).astype(BF16)


def mixer_kernel(x, dt, taps_in, bias_in, step_in, rate_in, skip_in, gain_in,
                 y_ref, scale_ref, gain_ref,
                 raw, raw_bc, dts, halo, taps, biases, vectors, sel, ext, keys, left, source, decay_2,
                 carry_2, vec_2, my_decay, decays, before_2, z_buf, p_buf, a_buf, a_out, h_buf, h_out,
                 y_out, squares,
                 xsend, xrecv, bsend, brecv, psend, precv, tsend, trecv, dsend, drecv, csend, crecv,
                 hsend, hrecv, osend, orecv, xown, own_sem):
    f, c, g, z, nz, nf, seg = place()
    last = nz * nf - 1
    rows = x.shape[0]
    chunks = raw.shape[0]
    gw = chunks * WIDTH
    di = gw * GROUPS
    heads = dt.shape[1]
    own = taps_in.shape[1]

    def peer(d):
        return {"fsdp": f, "ctx": z * GROUPS + lax.rem(g + d, GROUPS)}

    def sibling(d):
        return {"fsdp": lax.rem(f + d, nf), "ctx": c}

    def along(half, k):
        return {"fsdp": half, "ctx": k * GROUPS + g}

    sends_halo = jnp.logical_and(g == GROUPS - 1, seg < last)
    sends_half = jnp.logical_and(z == nz - 1, f < nf - 1)

    barrier = pltpu.get_barrier_semaphore()
    for d in range(1, GROUPS):
        pl.semaphore_signal(barrier, inc=1, device_id=peer(d))
    for d in range(1, nf):
        pl.semaphore_signal(barrier, inc=1, device_id=sibling(d))

    @pl.when(seg > 0)
    def _():
        pl.semaphore_signal(barrier, inc=1, device_id=device(seg - 1, GROUPS - 1, nz))

    for k in range(nz - 1):
        @pl.when(k < z)
        def _():
            pl.semaphore_signal(barrier, inc=1, device_id=along(f, k))

    @pl.when(f > 0)
    def _():
        pl.semaphore_signal(barrier, inc=1, device_id=along(f - 1, nz - 1))

    more = (nz - 1 - z) + jnp.where(sends_halo, GROUPS, 0) + jnp.where(sends_half, nz, 0)
    pl.semaphore_wait(barrier, GROUPS - 1 + nf - 1 + more)

    def b_at(p):
        return pl.ds(pl.multiple_of(di + p * N, 128), N)

    def c_at(p):
        return pl.ds(pl.multiple_of(di + (GROUPS + p) * N, 128), N)

    mine = pl.ds(pl.multiple_of(g * rows, 128), rows)

    def halo_copies():
        out = []
        tail = pl.ds(rows - HALO, HALO)
        for p in range(GROUPS):
            parts = [(x.at[tail, lanes(p, gw)], halo.at[:, 0:gw]),
                     (x.at[tail, b_at(p)], halo.at[:, gw : gw + N]),
                     (x.at[tail, c_at(p)], halo.at[:, gw + N : gw + 2 * N])]
            for k, (src, dst) in enumerate(parts):
                out.append(pltpu.make_async_remote_copy(
                    src, dst, tsend.at[p, k], trecv.at[k], device_id=device(seg + 1, p, nz)))
        return out

    @pl.when(sends_halo)
    def _():
        for copy in halo_copies():
            copy.start()

    params = [(taps_in, taps.at[:, lanes(f, own)]), (bias_in, biases.at[f]), (step_in, vectors.at[0, f]),
              (rate_in, vectors.at[1, f]), (skip_in, vectors.at[2, f]), (gain_in, gain_ref.at[f])]

    def small(p):
        return [(x.at[:, b_at(p)], raw_bc.at[mine, 0:N]),
                (x.at[:, c_at(p)], raw_bc.at[mine, N : 2 * N]), (dt, dts.at[g])]

    first = []
    for d in (2, 1, 3):
        for k, (src, dst) in enumerate(small(lax.rem(g + d, GROUPS))):
            first.append(pltpu.make_async_remote_copy(
                src, dst, bsend.at[d, k], brecv.at[d, k], device_id=peer(d)))
    for d in range(1, nf):
        for k, (src, dst) in enumerate(params):
            first.append(pltpu.make_async_remote_copy(
                src, dst, psend.at[d, k], precv.at[d, k], device_id=sibling(d)))
    for k, (src, dst) in enumerate(small(g) + params):
        first.append(pltpu.make_async_copy(src, dst, own_sem.at[k]))
    for copy in first:
        copy.start()

    def pieces(q):
        out = []
        for d in (2, 1, 3):
            p = lax.rem(g + d, GROUPS)
            out.append(pltpu.make_async_remote_copy(
                x.at[:, lanes(p * chunks + q, WIDTH)], raw.at[q, mine], xsend.at[d, q],
                xrecv.at[d, q], device_id=peer(d)))
        out.append(pltpu.make_async_copy(
            x.at[:, lanes(g * chunks + q, WIDTH)], raw.at[q, mine], xown.at[q]))
        return out

    @pl.loop(0, chunks)
    def _(q):
        for copy in pieces(q):
            copy.start()

    @pl.when(z == 0)
    def _():
        a_buf[...] = jnp.zeros_like(a_buf)

    @pl.when(f == 0)
    def _():
        h_buf[...] = jnp.zeros_like(h_buf)

    for k in range(nz - 1):
        @pl.when(k >= z)
        def _():
            decays[k] = jnp.ones((8, heads), F32)

    fill_selection(sel, g)
    squares[...] = jnp.zeros_like(squares)
    for copy in first:
        copy.wait()

    @pl.when(seg > 0)
    def _():
        for copy in halo_copies()[:3]:
            copy.wait_recv()

    def before(at, size):
        return jnp.where(seg > 0, halo[HALO - 8 :, at].astype(F32), 0.0)

    per_bias = own // 128

    def bias_of(i):
        return biases[i // per_bias, pl.ds(lax.rem(i, per_bias), 1), :]

    ext[0:8, :] = before(pl.ds(gw, 2 * N), 2 * N)
    ext[8:, :] = raw_bc[...].astype(F32)
    keys[...] = silu_conv(ext, 0, taps, bias_of(di // N + g), b_at(g), N)
    queries = silu_conv(ext, N, taps, bias_of(di // N + GROUPS + g), c_at(g), N)
    step_bias, rate_log, direct = (
        jnp.concatenate([vectors[k, i] for i in range(nf)], axis=1) for k in range(3))
    lower = (lax.broadcasted_iota(jnp.int32, (rows, rows), 0)
             >= lax.broadcasted_iota(jnp.int32, (rows, rows), 1))
    ones = jnp.where(lower, 1.0, 0.0)
    scale = jnp.exp(rate_log)
    decayed = jnp.ones((1, heads), F32)
    for j in range(GROUPS):
        at = pl.ds(j * rows, rows)
        delta = dts[j].astype(F32) + step_bias
        delta = jnp.maximum(delta, 0.0) + jnp.log1p(jnp.exp(-jnp.abs(delta)))
        cum = lax.dot_general(ones, -scale * delta, (((1,), (0,)), ((), ())),
                              precision=lax.Precision.HIGHEST, preferred_element_type=F32)
        decay = jnp.exp(cum)
        source[j] = hi_lo(delta * jnp.exp(-cum))
        decay_2[j] = hi_lo(decay)
        carry_2[j] = hi_lo(decay * decayed)
        block_decay = decay[rows - 1 : rows, :]
        decayed = decayed * block_decay
        vec_2[j] = hi_lo(jnp.concatenate(
            [direct, block_decay, decayed, jnp.zeros((5, heads), F32)], axis=0))
        mine_q = queries[j * rows : (j + 1) * rows]
        scores = jnp.where(lower, dot(mine_q, keys[at, :], ((1,), (1,))), 0.0).astype(BF16)
        left[j] = jnp.concatenate([scores, mine_q], axis=1)
    my_decay[...] = jnp.broadcast_to(decayed, (8, heads))

    def decay_copy(source_z, target_z):
        return pltpu.make_async_remote_copy(
            my_decay, decays.at[source_z], dsend.at[target_z], drecv.at[source_z],
            device_id=along(f, target_z))

    for k in range(1, nz):
        @pl.when(k > z)
        def _():
            decay_copy(z, k).start()

    def local_step(q):
        for copy in pieces(q)[:3]:
            copy.wait_recv()
        pieces(q)[3].wait()
        here = lanes(q, WIDTH)
        ext[0:8, :] = before(here, WIDTH)
        ext[8:, :] = raw[q].astype(F32)
        i = g * chunks + q
        bias = jnp.concatenate([bias_of(2 * i), bias_of(2 * i + 1)], axis=1)
        act = silu_conv(ext, 0, taps, bias, lanes(i, WIDTH), WIDTH)
        pick = sel[:, here]
        state = jnp.zeros((N, WIDTH), F32)
        for j in range(GROUPS):
            values = act[j * rows : (j + 1) * rows].astype(F32)
            weighted = (values * dot(source[j], pick)).astype(BF16)
            vec = dot(vec_2[j], pick)
            inner = dot(left[j], jnp.concatenate([weighted, state.astype(BF16)], axis=0))
            z_buf[q, j] = dot(decay_2[j], pick) * inner + vec[0:1, :] * values
            state = vec[1:2, :] * (state + dot(keys[pl.ds(j * rows, rows), :], weighted, ((0,), (0,))))
        p_buf[q] = state

    def hop(q):
        return pltpu.make_async_remote_copy(
            a_out.at[q], a_buf.at[q], csend.at[q], crecv.at[q], device_id=along(f, z + 1))

    def half(q, k):
        return pltpu.make_async_remote_copy(
            h_out.at[q], h_buf.at[q], hsend.at[k, q], hrecv.at[q], device_id=along(f + 1, k))

    def back(d, q):
        return pltpu.make_async_remote_copy(
            y_out.at[lax.rem(g + d, GROUPS), q], y_ref.at[:, lanes(g * chunks + q, WIDTH)],
            osend.at[d, q], orecv.at[d, q], device_id=peer(d))

    def through(pick):
        return dot(vec_2[GROUPS - 1], pick)[2:3, :]

    def chain_step(q):
        @pl.when(z > 0)
        def _():
            hop(q).wait_recv()

        @pl.when(z < nz - 1)
        def _():
            pick = sel[:, lanes(q, WIDTH)]
            a_out[q] = (p_buf[q] + through(pick) * a_buf[q].astype(F32)).astype(a_out.dtype)
            hop(q).start()

    def carry_step(q):
        pick = sel[:, lanes(q, WIDTH)]

        @pl.when(f > 0)
        def _():
            half(q, 0).wait_recv()

        state = a_buf[q].astype(F32) + dot(before_2[...], pick)[0:1, :] * h_buf[q].astype(F32)

        @pl.when(sends_half)
        def _():
            h_out[q] = (p_buf[q] + through(pick) * state).astype(h_out.dtype)
            for k in range(nz):
                half(q, k).start()

        low = state.astype(BF16)
        for j in range(GROUPS):
            carried = dot(left[j, :, N:], low) * dot(carry_2[j], pick)
            y_out[j, q] = (z_buf[q, j] + carried).astype(BF16)
        for d in range(1, GROUPS):
            back(d, q).start()
        y_ref[:, lanes(g * chunks + q, WIDTH)] = y_out[g, q]

    def bounded(v):
        return jnp.where(v < chunks, v, chunks)

    chain_lag = bounded(z)
    carry_lag = bounded(jnp.where(f == 0, z, nz - 1 + f))
    steps = chunks + min(chunks, nz - 1 + nf - 1)

    @pl.loop(0, steps)
    def _(i):
        @pl.when(i < chunks)
        def _():
            local_step(i)

        @pl.when(i == chain_lag)
        def _():
            product = jnp.ones((8, heads), F32)
            for k in range(nz - 1):
                @pl.when(k < z)
                def _():
                    decay_copy(k, k).wait_recv()

                product = product * decays[k]
            before_2[...] = hi_lo(product)

        @pl.when(jnp.logical_and(i >= chain_lag, i < chain_lag + chunks))
        def _():
            chain_step(i - chain_lag)

        @pl.when(jnp.logical_and(i >= carry_lag, i < carry_lag + chunks))
        def _():
            carry_step(i - carry_lag)

    @pl.loop(0, chunks)
    def _(q):
        for d in range(1, GROUPS):
            back(d, q).wait_recv()
        for p in range(GROUPS):
            y = y_ref[:, lanes(p * chunks + q, WIDTH)].astype(F32)
            squares[p] = squares[p] + y * y

    for p in range(GROUPS):
        norm = lax.rsqrt(jnp.sum(squares[p], axis=1, keepdims=True) * (1.0 / gw) + 1e-05)
        scale_ref[:, p * 128 : (p + 1) * 128] = jnp.broadcast_to(norm, (rows, 128))

    @pl.loop(0, chunks)
    def _(q):
        for copy in pieces(q)[:3]:
            copy.wait_send()
        for d in range(1, GROUPS):
            back(d, q).wait_send()

    @pl.when(z < nz - 1)
    def _():
        @pl.loop(0, chunks)
        def _(q):
            hop(q).wait_send()

    @pl.when(sends_half)
    def _():
        @pl.loop(0, chunks)
        def _(q):
            for k in range(nz):
                half(q, k).wait_send()

    for k in range(1, nz):
        @pl.when(k > z)
        def _():
            decay_copy(z, k).wait_send()

    @pl.when(sends_halo)
    def _():
        for copy in halo_copies():
            copy.wait_send()


def mixer(x, dt, taps, bias, step, rate, skip, gain):
    rows, ch = x.shape
    heads = dt.shape[1]
    nf = lax.axis_size("fsdp")
    nz = lax.axis_size("ctx") // GROUPS
    gw = heads * P_SIZE // GROUPS
    chunks = gw // WIDTH
    length = rows * GROUPS
    link = BF16 if nf * nz <= 8 else F32
    vm, dma = pltpu.VMEM, pltpu.SemaphoreType.DMA
    return pl.pallas_call(
        mixer_kernel,
        out_shape=(jax.ShapeDtypeStruct((rows, gw * GROUPS), BF16),
                   jax.ShapeDtypeStruct((rows, GROUPS * 128), F32),
                   jax.ShapeDtypeStruct((nf,) + gain.shape, F32)),
        in_specs=[HBM] * 8,
        out_specs=(WHOLE,) * 3,
        scratch_shapes=[
            vm((chunks, length, WIDTH), BF16),
            vm((length, 2 * N), BF16),
            vm((GROUPS, rows, heads), BF16),
            vm((HALO, gw + 2 * N), BF16),
            vm((4, ch), F32),
            vm((nf,) + bias.shape, F32),
            vm((3, nf) + step.shape, F32),
            vm((2 * heads, gw), BF16),
            vm((8 + length, WIDTH), F32),
            vm((length, N), BF16),
            vm((GROUPS, rows, 2 * N), BF16),
            vm((GROUPS, rows, 2 * heads), BF16),
            vm((GROUPS, rows, 2 * heads), BF16),
            vm((GROUPS, rows, 2 * heads), BF16),
            vm((GROUPS, 8, 2 * heads), BF16),
            vm((8, heads), F32),
            vm((nz, 8, heads), F32),
            vm((8, 2 * heads), BF16),
            vm((chunks, GROUPS, rows, WIDTH), F32),
            vm((chunks, N, WIDTH), F32),
            vm((chunks, N, WIDTH), link),
            vm((chunks, N, WIDTH), link),
            vm((chunks, N, WIDTH), link),
            vm((chunks, N, WIDTH), link),
            vm((GROUPS, chunks, rows, WIDTH), BF16),
            vm((GROUPS, rows, WIDTH), F32),
            dma((GROUPS, chunks)), dma((GROUPS, chunks)), dma((GROUPS, 3)), dma((GROUPS, 3)),
            dma((nf, 6)), dma((nf, 6)), dma((GROUPS, 3)), dma((3,)), dma((nz,)), dma((nz,)),
            dma((chunks,)), dma((chunks,)), dma((nz, chunks)), dma((chunks,)),
            dma((GROUPS, chunks)), dma((GROUPS, chunks)), dma((chunks,)), dma((9,)),
        ],
        compiler_params=pltpu.CompilerParams(
            collective_id=0, has_side_effects=True, vmem_limit_bytes=58 << 20),
        name="mixer",
    )(x, dt, taps, bias, step, rate, skip, gain)


def norm_kernel(y, scale, gain, out, buf, sem):
    gw = y.shape[1] // GROUPS
    own = gain.shape[2]
    copies = []
    for p in range(GROUPS):
        factor = scale[:, p * 128 : (p + 1) * 128]
        for at in range(p * gw, (p + 1) * gw, 128):
            gains = gain[at // own, :, at % own : at % own + 128]
            buf[:, at : at + 128] = (y[:, at : at + 128].astype(F32) * factor * gains).astype(BF16)
        here = slice(p * gw, (p + 1) * gw)
        copies.append(pltpu.make_async_copy(buf.at[:, here], out.at[:, here], sem.at[p]))
        copies[-1].start()
    for copy in copies:
        copy.wait()


def norm(y, scale, gain):
    return pl.pallas_call(
        norm_kernel,
        out_shape=jax.ShapeDtypeStruct(y.shape, BF16),
        in_specs=[WHOLE] * 3,
        out_specs=HBM,
        scratch_shapes=[pltpu.VMEM(y.shape, BF16), pltpu.SemaphoreType.DMA((GROUPS,))],
        compiler_params=pltpu.CompilerParams(vmem_limit_bytes=16 << 20),
        name="norm",
    )(y, scale, gain)


def local(xbc, dt, conv_weight, conv_bias, dt_bias, a_log, skip, norm_gain):
    y, scale, gain = mixer(
        xbc, dt, conv_weight, conv_bias.reshape(-1, 128), dt_bias.reshape(1, -1), a_log.reshape(1, -1),
        skip.reshape(1, -1), norm_gain.reshape(1, -1))
    return norm(y, scale, gain)


def solution(mesh):
    placed = (
        P(("fsdp", "ctx"), None),
        P(("fsdp", "ctx"), None),
        P(None, "fsdp"),
        P("fsdp"),
        P("fsdp"),
        P("fsdp"),
        P("fsdp"),
        P("fsdp"),
    )
    return jax.shard_map(
        local, mesh=mesh, in_specs=placed, out_specs=P(("fsdp", "ctx"), None), check_vma=False
    )
```

```python
import jax
import jax.numpy as jnp
from jax import lax
from jax.experimental import pallas as pl
from jax.experimental.pallas import tpu as pltpu
from jax.sharding import PartitionSpec as P

P_SIZE = 64
N = 128
GROUPS = 4
HALO = 16
WIDTH = 256
F32, BF16 = jnp.float32, jnp.bfloat16
HBM = pl.BlockSpec(memory_space=pltpu.HBM)
WHOLE = pl.BlockSpec(memory_space=pltpu.VMEM)


def place():
    f, c = lax.axis_index("fsdp"), lax.axis_index("ctx")
    nz = lax.axis_size("ctx") // GROUPS
    nf = lax.axis_size("fsdp")
    g, z = lax.rem(c, GROUPS), c // GROUPS
    return f, c, g, z, nz, nf, f * nz + z


def device(seg, g, nz):
    return {"fsdp": seg // nz, "ctx": lax.rem(seg, nz) * GROUPS + g}


def lanes(index, size):
    return pl.ds(pl.multiple_of(index * size, 128), size)


def hi_lo(v):
    hi = v.astype(BF16)
    return jnp.concatenate([hi, (v - hi.astype(F32)).astype(BF16)], axis=1)


def dot(a, b, dims=((1,), (0,))):
    return lax.dot_general(a, b, (dims, ((), ())), preferred_element_type=F32)


def fill_selection(sel, g):
    heads, width = sel.shape[0] // 2, sel.shape[1]
    per_group = width // P_SIZE
    row = lax.broadcasted_iota(jnp.int32, sel.shape, 0)
    col = lax.broadcasted_iota(jnp.int32, sel.shape, 1)
    row = jnp.where(row >= heads, row - heads, row)
    sel[...] = jnp.where(row == g * per_group + col // P_SIZE, 1.0, 0.0).astype(BF16)


def silu_conv(ext, start, taps, bias, at, size):
    rows = ext.shape[0] - 8
    total = bias
    for k in range(4):
        total = total + taps[k : k + 1, at] * ext[5 + k : 5 + k + rows, start : start + size]
    return (total / (1.0 + jnp.exp(-total))).astype(BF16)


def mixer_kernel(x, dt, taps_in, bias_in, step_in, rate_in, skip_in, gain_in,
                 y_ref, scale_ref, gain_ref,
                 raw, raw_bc, dts, halo, taps, biases, vectors, sel, ext, keys, left, source, decay_2,
                 carry_2, vec_2, my_decay, decays, before_2, z_buf, p_buf, a_buf, a_out, h_buf, h_out,
                 y_out, squares,
                 xsend, xrecv, bsend, brecv, psend, precv, tsend, trecv, dsend, drecv, csend, crecv,
                 hsend, hrecv, osend, orecv, xown, own_sem):
    f, c, g, z, nz, nf, seg = place()
    last = nz * nf - 1
    rows = x.shape[0]
    chunks = raw.shape[0]
    gw = chunks * WIDTH
    di = gw * GROUPS
    heads = dt.shape[1]
    own = taps_in.shape[1]

    def peer(d):
        return {"fsdp": f, "ctx": z * GROUPS + lax.rem(g + d, GROUPS)}

    def sibling(d):
        return {"fsdp": lax.rem(f + d, nf), "ctx": c}

    def along(half, k):
        return {"fsdp": half, "ctx": k * GROUPS + g}

    sends_halo = jnp.logical_and(g == GROUPS - 1, seg < last)
    sends_half = jnp.logical_and(z == nz - 1, f < nf - 1)

    barrier = pltpu.get_barrier_semaphore()
    for d in range(1, GROUPS):
        pl.semaphore_signal(barrier, inc=1, device_id=peer(d))
    for d in range(1, nf):
        pl.semaphore_signal(barrier, inc=1, device_id=sibling(d))

    @pl.when(seg > 0)
    def _():
        pl.semaphore_signal(barrier, inc=1, device_id=device(seg - 1, GROUPS - 1, nz))

    for k in range(nz - 1):
        @pl.when(k < z)
        def _():
            pl.semaphore_signal(barrier, inc=1, device_id=along(f, k))

    @pl.when(f > 0)
    def _():
        pl.semaphore_signal(barrier, inc=1, device_id=along(f - 1, nz - 1))

    more = (nz - 1 - z) + jnp.where(sends_halo, GROUPS, 0) + jnp.where(sends_half, nz, 0)
    pl.semaphore_wait(barrier, GROUPS - 1 + nf - 1 + more)

    def b_at(p):
        return pl.ds(pl.multiple_of(di + p * N, 128), N)

    def c_at(p):
        return pl.ds(pl.multiple_of(di + (GROUPS + p) * N, 128), N)

    mine = pl.ds(pl.multiple_of(g * rows, 128), rows)

    def halo_copies():
        out = []
        tail = pl.ds(rows - HALO, HALO)
        for p in range(GROUPS):
            parts = [(x.at[tail, lanes(p, gw)], halo.at[:, 0:gw]),
                     (x.at[tail, b_at(p)], halo.at[:, gw : gw + N]),
                     (x.at[tail, c_at(p)], halo.at[:, gw + N : gw + 2 * N])]
            for k, (src, dst) in enumerate(parts):
                out.append(pltpu.make_async_remote_copy(
                    src, dst, tsend.at[p, k], trecv.at[k], device_id=device(seg + 1, p, nz)))
        return out

    @pl.when(sends_halo)
    def _():
        for copy in halo_copies():
            copy.start()

    params = [(taps_in, taps.at[:, lanes(f, own)]), (bias_in, biases.at[f]), (step_in, vectors.at[0, f]),
              (rate_in, vectors.at[1, f]), (skip_in, vectors.at[2, f]), (gain_in, gain_ref.at[f])]

    def small(p):
        return [(x.at[:, b_at(p)], raw_bc.at[mine, 0:N]),
                (x.at[:, c_at(p)], raw_bc.at[mine, N : 2 * N]), (dt, dts.at[g])]

    first = []
    for d in (2, 1, 3):
        for k, (src, dst) in enumerate(small(lax.rem(g + d, GROUPS))):
            first.append(pltpu.make_async_remote_copy(
                src, dst, bsend.at[d, k], brecv.at[d, k], device_id=peer(d)))
    for d in range(1, nf):
        for k, (src, dst) in enumerate(params):
            first.append(pltpu.make_async_remote_copy(
                src, dst, psend.at[d, k], precv.at[d, k], device_id=sibling(d)))
    for k, (src, dst) in enumerate(small(g) + params):
        first.append(pltpu.make_async_copy(src, dst, own_sem.at[k]))
    for copy in first:
        copy.start()

    def pieces(q):
        out = []
        for d in (2, 1, 3):
            p = lax.rem(g + d, GROUPS)
            out.append(pltpu.make_async_remote_copy(
                x.at[:, lanes(p * chunks + q, WIDTH)], raw.at[q, mine], xsend.at[d, q],
                xrecv.at[d, q], device_id=peer(d)))
        out.append(pltpu.make_async_copy(
            x.at[:, lanes(g * chunks + q, WIDTH)], raw.at[q, mine], xown.at[q]))
        return out

    @pl.loop(0, chunks)
    def _(q):
        for copy in pieces(q):
            copy.start()

    @pl.when(z == 0)
    def _():
        a_buf[...] = jnp.zeros_like(a_buf)

    @pl.when(f == 0)
    def _():
        h_buf[...] = jnp.zeros_like(h_buf)

    for k in range(nz - 1):
        @pl.when(k >= z)
        def _():
            decays[k] = jnp.ones((8, heads), F32)

    fill_selection(sel, g)
    squares[...] = jnp.zeros_like(squares)
    for copy in first:
        copy.wait()

    @pl.when(seg > 0)
    def _():
        for copy in halo_copies()[:3]:
            copy.wait_recv()

    def before(at, size):
        return jnp.where(seg > 0, halo[HALO - 8 :, at].astype(F32), 0.0)

    per_bias = own // 128

    def bias_of(i):
        return biases[i // per_bias, pl.ds(lax.rem(i, per_bias), 1), :]

    ext[0:8, :] = before(pl.ds(gw, 2 * N), 2 * N)
    ext[8:, :] = raw_bc[...].astype(F32)
    keys[...] = silu_conv(ext, 0, taps, bias_of(di // N + g), b_at(g), N)
    queries = silu_conv(ext, N, taps, bias_of(di // N + GROUPS + g), c_at(g), N)
    step_bias, rate_log, direct = (
        jnp.concatenate([vectors[k, i] for i in range(nf)], axis=1) for k in range(3))
    lower = (lax.broadcasted_iota(jnp.int32, (rows, rows), 0)
             >= lax.broadcasted_iota(jnp.int32, (rows, rows), 1))
    ones = jnp.where(lower, 1.0, 0.0)
    scale = jnp.exp(rate_log)
    decayed = jnp.ones((1, heads), F32)
    for j in range(GROUPS):
        at = pl.ds(j * rows, rows)
        delta = dts[j].astype(F32) + step_bias
        delta = jnp.maximum(delta, 0.0) + jnp.log1p(jnp.exp(-jnp.abs(delta)))
        cum = lax.dot_general(ones, -scale * delta, (((1,), (0,)), ((), ())),
                              precision=lax.Precision.HIGHEST, preferred_element_type=F32)
        decay = jnp.exp(cum)
        source[j] = hi_lo(delta * jnp.exp(-cum))
        decay_2[j] = hi_lo(decay)
        carry_2[j] = hi_lo(decay * decayed)
        block_decay = decay[rows - 1 : rows, :]
        decayed = decayed * block_decay
        vec_2[j] = hi_lo(jnp.concatenate(
            [direct, block_decay, decayed, jnp.zeros((5, heads), F32)], axis=0))
        mine_q = queries[j * rows : (j + 1) * rows]
        scores = jnp.where(lower, dot(mine_q, keys[at, :], ((1,), (1,))), 0.0).astype(BF16)
        left[j] = jnp.concatenate([scores, mine_q], axis=1)
    my_decay[...] = jnp.broadcast_to(decayed, (8, heads))

    def decay_copy(source_z, target_z):
        return pltpu.make_async_remote_copy(
            my_decay, decays.at[source_z], dsend.at[target_z], drecv.at[source_z],
            device_id=along(f, target_z))

    for k in range(1, nz):
        @pl.when(k > z)
        def _():
            decay_copy(z, k).start()

    def local_step(q):
        for copy in pieces(q)[:3]:
            copy.wait_recv()
        pieces(q)[3].wait()
        here = lanes(q, WIDTH)
        ext[0:8, :] = before(here, WIDTH)
        ext[8:, :] = raw[q].astype(F32)
        i = g * chunks + q
        bias = jnp.concatenate([bias_of(2 * i), bias_of(2 * i + 1)], axis=1)
        act = silu_conv(ext, 0, taps, bias, lanes(i, WIDTH), WIDTH)
        pick = sel[:, here]
        state = jnp.zeros((N, WIDTH), F32)
        for j in range(GROUPS):
            values = act[j * rows : (j + 1) * rows].astype(F32)
            weighted = (values * dot(source[j], pick)).astype(BF16)
            vec = dot(vec_2[j], pick)
            inner = dot(left[j], jnp.concatenate([weighted, state.astype(BF16)], axis=0))
            z_buf[q, j] = dot(decay_2[j], pick) * inner + vec[0:1, :] * values
            state = vec[1:2, :] * (state + dot(keys[pl.ds(j * rows, rows), :], weighted, ((0,), (0,))))
        p_buf[q] = state

    def hop(q):
        return pltpu.make_async_remote_copy(
            a_out.at[q], a_buf.at[q], csend.at[q], crecv.at[q], device_id=along(f, z + 1))

    def half(q, k):
        return pltpu.make_async_remote_copy(
            h_out.at[q], h_buf.at[q], hsend.at[k, q], hrecv.at[q], device_id=along(f + 1, k))

    def back(d, q):
        return pltpu.make_async_remote_copy(
            y_out.at[lax.rem(g + d, GROUPS), q], y_ref.at[:, lanes(g * chunks + q, WIDTH)],
            osend.at[d, q], orecv.at[d, q], device_id=peer(d))

    def through(pick):
        return dot(vec_2[GROUPS - 1], pick)[2:3, :]

    def chain_step(q):
        @pl.when(z > 0)
        def _():
            hop(q).wait_recv()

        @pl.when(z < nz - 1)
        def _():
            pick = sel[:, lanes(q, WIDTH)]
            a_out[q] = (p_buf[q] + through(pick) * a_buf[q].astype(F32)).astype(a_out.dtype)
            hop(q).start()

    def carry_step(q):
        pick = sel[:, lanes(q, WIDTH)]

        @pl.when(f > 0)
        def _():
            half(q, 0).wait_recv()

        state = a_buf[q].astype(F32) + dot(before_2[...], pick)[0:1, :] * h_buf[q].astype(F32)

        @pl.when(sends_half)
        def _():
            h_out[q] = (p_buf[q] + through(pick) * state).astype(h_out.dtype)
            for k in range(nz):
                half(q, k).start()

        low = state.astype(BF16)
        for j in range(GROUPS):
            carried = dot(left[j, :, N:], low) * dot(carry_2[j], pick)
            y_out[j, q] = (z_buf[q, j] + carried).astype(BF16)
        for d in range(1, GROUPS):
            back(d, q).start()
        y_ref[:, lanes(g * chunks + q, WIDTH)] = y_out[g, q]

    def bounded(v):
        return jnp.where(v < chunks, v, chunks)

    chain_lag = bounded(z)
    carry_lag = bounded(jnp.where(f == 0, z, nz - 1 + f))
    steps = chunks + min(chunks, nz - 1 + nf - 1)

    @pl.loop(0, steps)
    def _(i):
        @pl.when(i < chunks)
        def _():
            local_step(i)

        @pl.when(i == chain_lag)
        def _():
            product = jnp.ones((8, heads), F32)
            for k in range(nz - 1):
                @pl.when(k < z)
                def _():
                    decay_copy(k, k).wait_recv()

                product = product * decays[k]
            before_2[...] = hi_lo(product)

        @pl.when(jnp.logical_and(i >= chain_lag, i < chain_lag + chunks))
        def _():
            chain_step(i - chain_lag)

        @pl.when(jnp.logical_and(i >= carry_lag, i < carry_lag + chunks))
        def _():
            carry_step(i - carry_lag)

    @pl.loop(0, chunks)
    def _(q):
        for d in range(1, GROUPS):
            back(d, q).wait_recv()
        for p in range(GROUPS):
            y = y_ref[:, lanes(p * chunks + q, WIDTH)].astype(F32)
            squares[p] = squares[p] + y * y

    for p in range(GROUPS):
        norm = lax.rsqrt(jnp.sum(squares[p], axis=1, keepdims=True) * (1.0 / gw) + 1e-05)
        scale_ref[:, p * 128 : (p + 1) * 128] = jnp.broadcast_to(norm, (rows, 128))

    @pl.loop(0, chunks)
    def _(q):
        for copy in pieces(q)[:3]:
            copy.wait_send()
        for d in range(1, GROUPS):
            back(d, q).wait_send()

    @pl.when(z < nz - 1)
    def _():
        @pl.loop(0, chunks)
        def _(q):
            hop(q).wait_send()

    @pl.when(sends_half)
    def _():
        @pl.loop(0, chunks)
        def _(q):
            for k in range(nz):
                half(q, k).wait_send()

    for k in range(1, nz):
        @pl.when(k > z)
        def _():
            decay_copy(z, k).wait_send()

    @pl.when(sends_halo)
    def _():
        for copy in halo_copies():
            copy.wait_send()


def mixer(x, dt, taps, bias, step, rate, skip, gain):
    rows, ch = x.shape
    heads = dt.shape[1]
    nf = lax.axis_size("fsdp")
    nz = lax.axis_size("ctx") // GROUPS
    gw = heads * P_SIZE // GROUPS
    chunks = gw // WIDTH
    length = rows * GROUPS
    link = BF16 if nf * nz <= 8 else F32
    vm, dma = pltpu.VMEM, pltpu.SemaphoreType.DMA
    return pl.pallas_call(
        mixer_kernel,
        out_shape=(jax.ShapeDtypeStruct((rows, gw * GROUPS), BF16),
                   jax.ShapeDtypeStruct((rows, GROUPS * 128), F32),
                   jax.ShapeDtypeStruct((nf,) + gain.shape, F32)),
        in_specs=[HBM] * 8,
        out_specs=(WHOLE,) * 3,
        scratch_shapes=[
            vm((chunks, length, WIDTH), BF16),
            vm((length, 2 * N), BF16),
            vm((GROUPS, rows, heads), BF16),
            vm((HALO, gw + 2 * N), BF16),
            vm((4, ch), F32),
            vm((nf,) + bias.shape, F32),
            vm((3, nf) + step.shape, F32),
            vm((2 * heads, gw), BF16),
            vm((8 + length, WIDTH), F32),
            vm((length, N), BF16),
            vm((GROUPS, rows, 2 * N), BF16),
            vm((GROUPS, rows, 2 * heads), BF16),
            vm((GROUPS, rows, 2 * heads), BF16),
            vm((GROUPS, rows, 2 * heads), BF16),
            vm((GROUPS, 8, 2 * heads), BF16),
            vm((8, heads), F32),
            vm((nz, 8, heads), F32),
            vm((8, 2 * heads), BF16),
            vm((chunks, GROUPS, rows, WIDTH), F32),
            vm((chunks, N, WIDTH), F32),
            vm((chunks, N, WIDTH), link),
            vm((chunks, N, WIDTH), link),
            vm((chunks, N, WIDTH), link),
            vm((chunks, N, WIDTH), link),
            vm((GROUPS, chunks, rows, WIDTH), BF16),
            vm((GROUPS, rows, WIDTH), F32),
            dma((GROUPS, chunks)), dma((GROUPS, chunks)), dma((GROUPS, 3)), dma((GROUPS, 3)),
            dma((nf, 6)), dma((nf, 6)), dma((GROUPS, 3)), dma((3,)), dma((nz,)), dma((nz,)),
            dma((chunks,)), dma((chunks,)), dma((nz, chunks)), dma((chunks,)),
            dma((GROUPS, chunks)), dma((GROUPS, chunks)), dma((chunks,)), dma((9,)),
        ],
        compiler_params=pltpu.CompilerParams(
            collective_id=0, has_side_effects=True, vmem_limit_bytes=51 << 20),
        name="mixer",
    )(x, dt, taps, bias, step, rate, skip, gain)


def norm_kernel(y, scale, gain, out, buf, sem):
    gw = y.shape[1] // GROUPS
    own = gain.shape[2]
    copies = []
    for p in range(GROUPS):
        factor = scale[:, p * 128 : (p + 1) * 128]
        for at in range(p * gw, (p + 1) * gw, 128):
            gains = gain[at // own, :, at % own : at % own + 128]
            buf[:, at : at + 128] = (y[:, at : at + 128].astype(F32) * factor * gains).astype(BF16)
        here = slice(p * gw, (p + 1) * gw)
        copies.append(pltpu.make_async_copy(buf.at[:, here], out.at[:, here], sem.at[p]))
        copies[-1].start()
    for copy in copies:
        copy.wait()


def norm(y, scale, gain):
    return pl.pallas_call(
        norm_kernel,
        out_shape=jax.ShapeDtypeStruct(y.shape, BF16),
        in_specs=[WHOLE] * 3,
        out_specs=HBM,
        scratch_shapes=[pltpu.VMEM(y.shape, BF16), pltpu.SemaphoreType.DMA((GROUPS,))],
        compiler_params=pltpu.CompilerParams(vmem_limit_bytes=16 << 20),
        name="norm",
    )(y, scale, gain)


def local(xbc, dt, conv_weight, conv_bias, dt_bias, a_log, skip, norm_gain):
    y, scale, gain = mixer(*(pltpu.with_memory_space_constraint(v, pltpu.HBM) for v in (
        xbc, dt, conv_weight, conv_bias.reshape(-1, 128), dt_bias.reshape(1, -1), a_log.reshape(1, -1),
        skip.reshape(1, -1), norm_gain.reshape(1, -1))))
    return norm(y, scale, gain)


def solution(mesh):
    placed = (
        P(("fsdp", "ctx"), None),
        P(("fsdp", "ctx"), None),
        P(None, "fsdp"),
        P("fsdp"),
        P("fsdp"),
        P("fsdp"),
        P("fsdp"),
        P("fsdp"),
    )
    return jax.shard_map(
        local, mesh=mesh, in_specs=placed, out_specs=P(("fsdp", "ctx"), None), check_vma=False
    )
```

```python
import jax
import jax.numpy as jnp
from jax import lax
from jax.experimental import pallas as pl
from jax.experimental.pallas import tpu as pltpu
from jax.sharding import PartitionSpec as P

P_SIZE = 64
N = 128
GROUPS = 4
HALO = 16
WIDTH = 256
F32, BF16 = jnp.float32, jnp.bfloat16
HBM = pl.BlockSpec(memory_space=pltpu.HBM)
WHOLE = pl.BlockSpec(memory_space=pltpu.VMEM)


def place():
    f, c = lax.axis_index("fsdp"), lax.axis_index("ctx")
    nz = lax.axis_size("ctx") // GROUPS
    nf = lax.axis_size("fsdp")
    g, z = lax.rem(c, GROUPS), c // GROUPS
    return f, c, g, z, nz, nf, f * nz + z


def device(seg, g, nz):
    return {"fsdp": seg // nz, "ctx": lax.rem(seg, nz) * GROUPS + g}


def lanes(index, size):
    return pl.ds(pl.multiple_of(index * size, 128), size)


def hi_lo(v):
    hi = v.astype(BF16)
    return jnp.concatenate([hi, (v - hi.astype(F32)).astype(BF16)], axis=1)


def dot(a, b, dims=((1,), (0,))):
    return lax.dot_general(a, b, (dims, ((), ())), preferred_element_type=F32)


def fill_selection(sel):
    heads = sel.shape[0] // 2
    row = lax.broadcasted_iota(jnp.int32, sel.shape, 0)
    col = lax.broadcasted_iota(jnp.int32, sel.shape, 1)
    row = jnp.where(row >= heads, row - heads, row)
    sel[...] = jnp.where(row == col // P_SIZE, 1.0, 0.0).astype(BF16)


def silu_conv(ext, start, taps, bias, at, size):
    rows = ext.shape[0] - 8
    total = bias
    for k in range(4):
        total = total + taps[k : k + 1, at] * ext[5 + k : 5 + k + rows, start : start + size]
    return (total / (1.0 + jnp.exp(-total))).astype(BF16)


def mixer_kernel(x, dt, taps_in, bias_in, step_in, rate_in, skip_in, gain_in,
                 y_ref, scale_ref, gain_ref,
                 raw, raw_bc, dt_own, dt_packs, dts, tail, packing, packs, halo, halos, taps, biases, vectors, sel, ext, keys, left, source, decay_2,
                 carry_2, vec_2, my_decay, decays, before_2, z_buf, p_buf, a_buf, a_out, h_buf, h_out,
                 y_out, squares,
                 xsend, xrecv, bsend, brecv, psend, precv, tsend, trecv, dsend, drecv, csend, crecv,
                 hsend, hrecv, osend, orecv, xown, own_sem):
    f, c, g, z, nz, nf, seg = place()
    last = nz * nf - 1
    rows = x.shape[0]
    chunks = raw.shape[0]
    gw = chunks * WIDTH
    di = gw * GROUPS
    heads = dt.shape[1]
    own = taps_in.shape[1]

    def peer(d):
        return {"fsdp": f, "ctx": z * GROUPS + lax.rem(g + d, GROUPS)}

    def sibling(d):
        return {"fsdp": lax.rem(f + d, nf), "ctx": c}

    def along(half, k):
        return {"fsdp": half, "ctx": k * GROUPS + g}

    sends_halo = jnp.logical_and(g == GROUPS - 1, seg < last)
    sends_half = jnp.logical_and(z == nz - 1, f < nf - 1)

    barrier = pltpu.get_barrier_semaphore()
    for d in range(1, GROUPS):
        pl.semaphore_signal(barrier, inc=1, device_id=peer(d))
    for d in range(1, nf):
        pl.semaphore_signal(barrier, inc=1, device_id=sibling(d))

    @pl.when(seg > 0)
    def _():
        pl.semaphore_signal(barrier, inc=1, device_id=device(seg - 1, GROUPS - 1, nz))

    for k in range(nz - 1):
        @pl.when(k < z)
        def _():
            pl.semaphore_signal(barrier, inc=1, device_id=along(f, k))

    @pl.when(f > 0)
    def _():
        pl.semaphore_signal(barrier, inc=1, device_id=along(f - 1, nz - 1))

    steps_in = pltpu.make_async_copy(dt, dt_own, own_sem.at[9])
    steps_in.start()

    @pl.when(sends_halo)
    def _():
        rows_in = pltpu.make_async_copy(x.at[pl.ds(rows - HALO, HALO), :], tail, own_sem.at[10])
        rows_in.start()
        packing[...] = jnp.zeros_like(packing)
        rows_in.wait()
        for p in range(GROUPS):
            starts = [p * gw + k * WIDTH for k in range(chunks)]
            for k, at in enumerate(starts):
                packing[3 * k : 3 * k + 3, :] = tail[:, at : at + WIDTH].astype(F32)[HALO - 3 :]
            for k, at in enumerate((di + p * N, di + (GROUPS + p) * N)):
                packing[3 * chunks : 3 * chunks + 3, k * N : (k + 1) * N] = (
                    tail[:, at : at + N].astype(F32)[HALO - 3 :])
            packs[p] = packing[...].astype(BF16)

    steps_in.wait()
    part = rows // GROUPS
    slot = lax.broadcasted_iota(jnp.int32, (part, heads), 1) // (heads // GROUPS)
    blocks = [dt_own[k * part : (k + 1) * part, :].astype(F32) for k in range(GROUPS)]
    for p in range(GROUPS):
        packed = jnp.zeros((part, heads), F32)
        for k in range(GROUPS):
            turned = pltpu.roll(blocks[k], (k - p) % GROUPS * (heads // GROUPS), 1)
            packed = jnp.where(slot == k, turned, packed)
        dt_packs[p] = packed.astype(BF16)

    more = (nz - 1 - z) + jnp.where(sends_halo, GROUPS, 0) + jnp.where(sends_half, nz, 0)
    pl.semaphore_wait(barrier, GROUPS - 1 + nf - 1 + more)

    def b_at(p):
        return pl.ds(pl.multiple_of(di + p * N, 128), N)

    def c_at(p):
        return pl.ds(pl.multiple_of(di + (GROUPS + p) * N, 128), N)

    mine = pl.ds(pl.multiple_of(g * rows, 128), rows)

    def halo_copies():
        return [pltpu.make_async_remote_copy(
            packs.at[p], halo, tsend.at[p], trecv.at[0], device_id=device(seg + 1, p, nz))
            for p in range(GROUPS)]

    @pl.when(sends_halo)
    def _():
        for copy in halo_copies():
            copy.start()

    params = [(taps_in, taps.at[:, lanes(f, own)]), (bias_in, biases.at[f]), (step_in, vectors.at[0, f]),
              (rate_in, vectors.at[1, f]), (skip_in, vectors.at[2, f]), (gain_in, gain_ref.at[f])]

    def small(p):
        return [(x.at[:, b_at(p)], raw_bc.at[mine, 0:N]),
                (x.at[:, c_at(p)], raw_bc.at[mine, N : 2 * N]), (dt_packs.at[p], dts.at[g])]

    first = []
    for d in (2, 1, 3):
        for k, (src, dst) in enumerate(small(lax.rem(g + d, GROUPS))):
            first.append(pltpu.make_async_remote_copy(
                src, dst, bsend.at[d, k], brecv.at[d, k], device_id=peer(d)))
    for d in range(1, nf):
        for k, (src, dst) in enumerate(params):
            first.append(pltpu.make_async_remote_copy(
                src, dst, psend.at[d, k], precv.at[d, k], device_id=sibling(d)))
    for k, (src, dst) in enumerate(small(g) + params):
        first.append(pltpu.make_async_copy(src, dst, own_sem.at[k]))
    for copy in first:
        copy.start()

    def pieces(q):
        out = []
        for d in (2, 1, 3):
            p = lax.rem(g + d, GROUPS)
            out.append(pltpu.make_async_remote_copy(
                x.at[:, lanes(p * chunks + q, WIDTH)], raw.at[q, mine], xsend.at[d, q],
                xrecv.at[d, q], device_id=peer(d)))
        out.append(pltpu.make_async_copy(
            x.at[:, lanes(g * chunks + q, WIDTH)], raw.at[q, mine], xown.at[q]))
        return out

    @pl.loop(0, chunks)
    def _(q):
        for copy in pieces(q):
            copy.start()

    @pl.when(z == 0)
    def _():
        a_buf[...] = jnp.zeros_like(a_buf)

    @pl.when(f == 0)
    def _():
        h_buf[...] = jnp.zeros_like(h_buf)

    for k in range(nz - 1):
        @pl.when(k >= z)
        def _():
            decays[k] = jnp.ones((8, heads), F32)

    fill_selection(sel)
    squares[...] = jnp.zeros_like(squares)
    halos[...] = jnp.zeros_like(halos)
    for copy in first:
        copy.wait()

    @pl.when(seg > 0)
    def _():
        halo_copies()[0].wait_recv()
        for k in range(chunks + 1):
            halos[k, 5:8, :] = halo[...].astype(F32)[3 * k : 3 * k + 3]

    per_bias = own // 128

    def bias_of(i):
        return biases[i // per_bias, pl.ds(lax.rem(i, per_bias), 1), :]

    ext[0:8, :] = halos[chunks]
    ext[8:, :] = raw_bc[...].astype(F32)
    keys[...] = silu_conv(ext, 0, taps, bias_of(di // N + g), b_at(g), N)
    queries = silu_conv(ext, N, taps, bias_of(di // N + GROUPS + g), c_at(g), N)
    to_front = lax.rem(GROUPS - g, GROUPS) * (heads // GROUPS)
    step_bias, rate_log, direct = (
        pltpu.roll(jnp.broadcast_to(jnp.concatenate([vectors[k, i] for i in range(nf)], axis=1), (8, heads)),
                   to_front, 1)[0:1] for k in range(3))
    lower = (lax.broadcasted_iota(jnp.int32, (rows, rows), 0)
             >= lax.broadcasted_iota(jnp.int32, (rows, rows), 1))
    ones = jnp.where(lower, 1.0, 0.0)
    scale = jnp.exp(rate_log)
    decayed = jnp.ones((1, heads), F32)
    for j in range(GROUPS):
        at = pl.ds(j * rows, rows)
        steps_of = dts[j].astype(F32)
        delta = jnp.concatenate(
            [pltpu.roll(steps_of, (GROUPS - k) % GROUPS * (heads // GROUPS), 1) for k in range(GROUPS)],
            axis=0) + step_bias
        delta = jnp.maximum(delta, 0.0) + jnp.log1p(jnp.exp(-jnp.abs(delta)))
        cum = lax.dot_general(ones, -scale * delta, (((1,), (0,)), ((), ())),
                              precision=lax.Precision.HIGHEST, preferred_element_type=F32)
        decay = jnp.exp(cum)
        source[j] = hi_lo(delta * jnp.exp(-cum))
        decay_2[j] = hi_lo(decay)
        carry_2[j] = hi_lo(decay * decayed)
        block_decay = decay[rows - 1 : rows, :]
        decayed = decayed * block_decay
        vec_2[j] = hi_lo(jnp.concatenate(
            [direct, block_decay, decayed, jnp.zeros((5, heads), F32)], axis=0))
        mine_q = queries[j * rows : (j + 1) * rows]
        scores = jnp.where(lower, dot(mine_q, keys[at, :], ((1,), (1,))), 0.0).astype(BF16)
        left[j] = jnp.concatenate([scores, mine_q], axis=1)
    my_decay[...] = jnp.broadcast_to(decayed, (8, heads))

    def decay_copy(source_z, target_z):
        return pltpu.make_async_remote_copy(
            my_decay, decays.at[source_z], dsend.at[target_z], drecv.at[source_z],
            device_id=along(f, target_z))

    for k in range(1, nz):
        @pl.when(k > z)
        def _():
            decay_copy(z, k).start()

    def local_step(q):
        for copy in pieces(q)[:3]:
            copy.wait_recv()
        pieces(q)[3].wait()
        here = lanes(q, WIDTH)
        ext[0:8, :] = halos[q]
        ext[8:, :] = raw[q].astype(F32)
        i = g * chunks + q
        bias = jnp.concatenate([bias_of(2 * i), bias_of(2 * i + 1)], axis=1)
        act = silu_conv(ext, 0, taps, bias, lanes(i, WIDTH), WIDTH)
        pick = sel[:, here]
        state = jnp.zeros((N, WIDTH), F32)
        for j in range(GROUPS):
            values = act[j * rows : (j + 1) * rows].astype(F32)
            weighted = (values * dot(source[j], pick)).astype(BF16)
            vec = dot(vec_2[j], pick)
            inner = dot(left[j], jnp.concatenate([weighted, state.astype(BF16)], axis=0))
            z_buf[q, j] = dot(decay_2[j], pick) * inner + vec[0:1, :] * values
            state = vec[1:2, :] * (state + dot(keys[pl.ds(j * rows, rows), :], weighted, ((0,), (0,))))
        p_buf[q] = state

    def hop(q):
        return pltpu.make_async_remote_copy(
            a_out.at[q], a_buf.at[q], csend.at[q], crecv.at[q], device_id=along(f, z + 1))

    def half(q, k):
        return pltpu.make_async_remote_copy(
            h_out.at[q], h_buf.at[q], hsend.at[k, q], hrecv.at[q], device_id=along(f + 1, k))

    def back(d, q):
        return pltpu.make_async_remote_copy(
            y_out.at[lax.rem(g + d, GROUPS), q], y_ref.at[:, lanes(g * chunks + q, WIDTH)],
            osend.at[d, q], orecv.at[d, q], device_id=peer(d))

    def through(pick):
        return dot(vec_2[GROUPS - 1], pick)[2:3, :]

    def chain_step(q):
        @pl.when(z > 0)
        def _():
            hop(q).wait_recv()

        @pl.when(z < nz - 1)
        def _():
            pick = sel[:, lanes(q, WIDTH)]
            a_out[q] = (p_buf[q] + through(pick) * a_buf[q].astype(F32)).astype(a_out.dtype)
            hop(q).start()

    def carry_step(q):
        pick = sel[:, lanes(q, WIDTH)]

        @pl.when(f > 0)
        def _():
            half(q, 0).wait_recv()

        state = a_buf[q].astype(F32) + dot(before_2[...], pick)[0:1, :] * h_buf[q].astype(F32)

        @pl.when(sends_half)
        def _():
            h_out[q] = (p_buf[q] + through(pick) * state).astype(h_out.dtype)
            for k in range(nz):
                half(q, k).start()

        low = state.astype(BF16)
        for j in range(GROUPS):
            carried = dot(left[j, :, N:], low) * dot(carry_2[j], pick)
            y_out[j, q] = (z_buf[q, j] + carried).astype(BF16)
        for d in range(1, GROUPS):
            back(d, q).start()
        y_ref[:, lanes(g * chunks + q, WIDTH)] = y_out[g, q]

    def bounded(v):
        return jnp.where(v < chunks, v, chunks)

    chain_lag = bounded(z)
    carry_lag = bounded(jnp.where(f == 0, z, nz - 1 + f))
    steps = chunks + min(chunks, nz - 1 + nf - 1)

    @pl.loop(0, steps)
    def _(i):
        @pl.when(i < chunks)
        def _():
            local_step(i)

        @pl.when(i == chain_lag)
        def _():
            product = jnp.ones((8, heads), F32)
            for k in range(nz - 1):
                @pl.when(k < z)
                def _():
                    decay_copy(k, k).wait_recv()

                product = product * decays[k]
            before_2[...] = hi_lo(product)

        @pl.when(jnp.logical_and(i >= chain_lag, i < chain_lag + chunks))
        def _():
            chain_step(i - chain_lag)

        @pl.when(jnp.logical_and(i >= carry_lag, i < carry_lag + chunks))
        def _():
            carry_step(i - carry_lag)

    @pl.loop(0, chunks)
    def _(q):
        for d in range(1, GROUPS):
            back(d, q).wait_recv()
        for p in range(GROUPS):
            y = y_ref[:, lanes(p * chunks + q, WIDTH)].astype(F32)
            squares[p] = squares[p] + y * y

    for p in range(GROUPS):
        norm = lax.rsqrt(jnp.sum(squares[p], axis=1, keepdims=True) * (1.0 / gw) + 1e-05)
        scale_ref[:, p * 128 : (p + 1) * 128] = jnp.broadcast_to(norm, (rows, 128))

    @pl.loop(0, chunks)
    def _(q):
        for copy in pieces(q)[:3]:
            copy.wait_send()
        for d in range(1, GROUPS):
            back(d, q).wait_send()

    @pl.when(z < nz - 1)
    def _():
        @pl.loop(0, chunks)
        def _(q):
            hop(q).wait_send()

    @pl.when(sends_half)
    def _():
        @pl.loop(0, chunks)
        def _(q):
            for k in range(nz):
                half(q, k).wait_send()

    for k in range(1, nz):
        @pl.when(k > z)
        def _():
            decay_copy(z, k).wait_send()

    @pl.when(sends_halo)
    def _():
        for copy in halo_copies():
            copy.wait_send()


def mixer(x, dt, taps, bias, step, rate, skip, gain):
    rows, ch = x.shape
    heads = dt.shape[1]
    nf = lax.axis_size("fsdp")
    nz = lax.axis_size("ctx") // GROUPS
    gw = heads * P_SIZE // GROUPS
    chunks = gw // WIDTH
    length = rows * GROUPS
    packed_rows = -(-3 * (chunks + 1) // 16) * 16
    link = BF16 if nf * nz <= 8 else F32
    vm, dma = pltpu.VMEM, pltpu.SemaphoreType.DMA
    return pl.pallas_call(
        mixer_kernel,
        out_shape=(jax.ShapeDtypeStruct((rows, gw * GROUPS), BF16),
                   jax.ShapeDtypeStruct((rows, GROUPS * 128), F32),
                   jax.ShapeDtypeStruct((nf,) + gain.shape, F32)),
        in_specs=[HBM] * 8,
        out_specs=(WHOLE,) * 3,
        scratch_shapes=[
            vm((chunks, length, WIDTH), BF16),
            vm((length, 2 * N), BF16),
            vm((rows, heads), BF16),
            vm((GROUPS, rows // GROUPS, heads), BF16),
            vm((GROUPS, rows // GROUPS, heads), BF16),
            vm((HALO, ch), BF16),
            vm((packed_rows, WIDTH), F32),
            vm((GROUPS, packed_rows, WIDTH), BF16),
            vm((packed_rows, WIDTH), BF16),
            vm((chunks + 1, 8, WIDTH), F32),
            vm((4, ch), F32),
            vm((nf,) + bias.shape, F32),
            vm((3, nf) + step.shape, F32),
            vm((2 * heads, gw), BF16),
            vm((8 + length, WIDTH), F32),
            vm((length, N), BF16),
            vm((GROUPS, rows, 2 * N), BF16),
            vm((GROUPS, rows, 2 * heads), BF16),
            vm((GROUPS, rows, 2 * heads), BF16),
            vm((GROUPS, rows, 2 * heads), BF16),
            vm((GROUPS, 8, 2 * heads), BF16),
            vm((8, heads), F32),
            vm((nz, 8, heads), F32),
            vm((8, 2 * heads), BF16),
            vm((chunks, GROUPS, rows, WIDTH), F32),
            vm((chunks, N, WIDTH), F32),
            vm((chunks, N, WIDTH), link),
            vm((chunks, N, WIDTH), link),
            vm((chunks, N, WIDTH), link),
            vm((chunks, N, WIDTH), link),
            vm((GROUPS, chunks, rows, WIDTH), BF16),
            vm((GROUPS, rows, WIDTH), F32),
            dma((GROUPS, chunks)), dma((GROUPS, chunks)), dma((GROUPS, 3)), dma((GROUPS, 3)),
            dma((nf, 6)), dma((nf, 6)), dma((GROUPS,)), dma((1,)), dma((nz,)), dma((nz,)),
            dma((chunks,)), dma((chunks,)), dma((nz, chunks)), dma((chunks,)),
            dma((GROUPS, chunks)), dma((GROUPS, chunks)), dma((chunks,)), dma((11,)),
        ],
        compiler_params=pltpu.CompilerParams(
            collective_id=0, has_side_effects=True, vmem_limit_bytes=51 << 20),
        name="mixer",
    )(x, dt, taps, bias, step, rate, skip, gain)


def norm_kernel(y, scale, gain, out, buf, sem):
    gw = y.shape[1] // GROUPS
    own = gain.shape[2]
    copies = []
    for p in range(GROUPS):
        factor = scale[:, p * 128 : (p + 1) * 128]
        for at in range(p * gw, (p + 1) * gw, 128):
            gains = gain[at // own, :, at % own : at % own + 128]
            buf[:, at : at + 128] = (y[:, at : at + 128].astype(F32) * factor * gains).astype(BF16)
        here = slice(p * gw, (p + 1) * gw)
        copies.append(pltpu.make_async_copy(buf.at[:, here], out.at[:, here], sem.at[p]))
        copies[-1].start()
    for copy in copies:
        copy.wait()


def norm(y, scale, gain):
    return pl.pallas_call(
        norm_kernel,
        out_shape=jax.ShapeDtypeStruct(y.shape, BF16),
        in_specs=[WHOLE] * 3,
        out_specs=HBM,
        scratch_shapes=[pltpu.VMEM(y.shape, BF16), pltpu.SemaphoreType.DMA((GROUPS,))],
        compiler_params=pltpu.CompilerParams(vmem_limit_bytes=16 << 20),
        name="norm",
    )(y, scale, gain)


def local(xbc, dt, conv_weight, conv_bias, dt_bias, a_log, skip, norm_gain):
    y, scale, gain = mixer(*(pltpu.with_memory_space_constraint(v, pltpu.HBM) for v in (
        xbc, dt, conv_weight, conv_bias.reshape(-1, 128), dt_bias.reshape(1, -1), a_log.reshape(1, -1),
        skip.reshape(1, -1), norm_gain.reshape(1, -1))))
    return norm(y, scale, gain)


def solution(mesh):
    placed = (
        P(("fsdp", "ctx"), None),
        P(("fsdp", "ctx"), None),
        P(None, "fsdp"),
        P("fsdp"),
        P("fsdp"),
        P("fsdp"),
        P("fsdp"),
        P("fsdp"),
    )
    return jax.shard_map(
        local, mesh=mesh, in_specs=placed, out_specs=P(("fsdp", "ctx"), None), check_vma=False
    )
```

```python
import jax
import jax.numpy as jnp
from jax import lax
from jax.experimental import pallas as pl
from jax.experimental.pallas import tpu as pltpu
from jax.sharding import PartitionSpec as P

P_SIZE = 64
N = 128
GROUPS = 4
HALO = 16
WIDTH = 256
F32, BF16 = jnp.float32, jnp.bfloat16
HBM = pl.BlockSpec(memory_space=pltpu.HBM)
WHOLE = pl.BlockSpec(memory_space=pltpu.VMEM)


def place():
    f, c = lax.axis_index("fsdp"), lax.axis_index("ctx")
    nz = lax.axis_size("ctx") // GROUPS
    nf = lax.axis_size("fsdp")
    g, z = lax.rem(c, GROUPS), c // GROUPS
    return f, c, g, z, nz, nf, f * nz + z


def device(seg, g, nz):
    return {"fsdp": seg // nz, "ctx": lax.rem(seg, nz) * GROUPS + g}


def lanes(index, size):
    return pl.ds(pl.multiple_of(index * size, 128), size)


def hi_lo(v):
    hi = v.astype(BF16)
    return jnp.concatenate([hi, (v - hi.astype(F32)).astype(BF16)], axis=1)


def dot(a, b, dims=((1,), (0,))):
    return lax.dot_general(a, b, (dims, ((), ())), preferred_element_type=F32)


def fill_selection(sel):
    heads = sel.shape[0] // 2
    row = lax.broadcasted_iota(jnp.int32, sel.shape, 0)
    col = lax.broadcasted_iota(jnp.int32, sel.shape, 1)
    row = jnp.where(row >= heads, row - heads, row)
    sel[...] = jnp.where(row == col // P_SIZE, 1.0, 0.0).astype(BF16)


def silu_conv(ext, start, taps, bias, at, size):
    rows = ext.shape[0] - 8
    total = bias
    for k in range(4):
        total = total + taps[k : k + 1, at] * ext[5 + k : 5 + k + rows, start : start + size]
    return (total / (1.0 + jnp.exp(-total))).astype(BF16)


def mixer_kernel(x, dt, taps_in, bias_in, step_in, rate_in, skip_in, gain_in,
                 y_ref, scale_ref, gain_ref,
                 raw, raw_bc, dt_own, dt_packs, dts, tail, packing, packs, halo, halos, taps, biases, vectors, sel, ext, keys, left, source, decay_2,
                 carry_2, vec_2, my_decay, next_decay, decays, before_2, z_buf, p_buf, a_buf, a_out, h_buf, h_out,
                 y_out, squares,
                 xsend, xrecv, bsend, brecv, psend, precv, tsend, trecv, dsend, drecv, csend, crecv,
                 hsend, hrecv, osend, orecv, xown, own_sem, chain_ready, plane_ready):
    f, c, g, z, nz, nf, seg = place()
    last = nz * nf - 1
    rows = x.shape[0]
    chunks = raw.shape[0]
    gw = chunks * WIDTH
    di = gw * GROUPS
    heads = dt.shape[1]
    own = taps_in.shape[1]

    def peer(d):
        return {"fsdp": f, "ctx": z * GROUPS + lax.rem(g + d, GROUPS)}

    def sibling(d):
        return {"fsdp": lax.rem(f + d, nf), "ctx": c}

    def along(half, k):
        return {"fsdp": half, "ctx": k * GROUPS + g}

    def tail_copy():
        return pltpu.make_async_copy(x.at[pl.ds(rows - HALO, HALO), :], tail, own_sem.at[10])

    sends_halo = jnp.logical_and(g == GROUPS - 1, seg < last)
    sends_half = jnp.logical_and(z == nz - 1, f < nf - 1)
    tells_plane = jnp.logical_and(g == GROUPS - 1, z < nz - 1)

    barrier = pltpu.get_barrier_semaphore()
    for d in range(1, GROUPS):
        pl.semaphore_signal(barrier, inc=1, device_id=peer(d))
    for d in range(1, nf):
        pl.semaphore_signal(barrier, inc=1, device_id=sibling(d))

    @pl.when(z < nz - 1)
    def _():
        pl.semaphore_signal(barrier, inc=1, device_id=along(f, z + 1))

    @pl.when(tells_plane)
    def _():
        for p in range(GROUPS):
            pl.semaphore_signal(barrier, inc=1, device_id=device(seg + 1, p, nz))

    @pl.when(f > 0)
    def _():
        pl.semaphore_signal(barrier, inc=1, device_id=along(f - 1, nz - 1))

    @pl.when(jnp.logical_and(f > 0, z == 0))
    def _():
        pl.semaphore_signal(barrier, inc=1, device_id=device(seg - 1, GROUPS - 1, nz))

    steps_in = pltpu.make_async_copy(dt, dt_own, own_sem.at[9])
    steps_in.start()

    @pl.when(sends_halo)
    def _():
        tail_copy().start()

    more = jnp.where(z > 0, 2, 0) + jnp.where(sends_half, jnp.where(g == GROUPS - 1, nz + GROUPS, nz), 0)
    pl.semaphore_wait(barrier, GROUPS - 1 + nf - 1 + more)

    def b_at(p):
        return pl.ds(pl.multiple_of(di + p * N, 128), N)

    def c_at(p):
        return pl.ds(pl.multiple_of(di + (GROUPS + p) * N, 128), N)

    mine = pl.ds(pl.multiple_of(g * rows, 128), rows)

    def halo_copies():
        return [pltpu.make_async_remote_copy(
            packs.at[p], halo, tsend.at[p], trecv.at[0], device_id=device(seg + 1, p, nz))
            for p in range(GROUPS)]

    params = [(taps_in, taps.at[:, lanes(f, own)]), (bias_in, biases.at[f]), (step_in, vectors.at[0, f]),
              (rate_in, vectors.at[1, f]), (skip_in, vectors.at[2, f]), (gain_in, gain_ref.at[f])]

    def states(p):
        return [(x.at[:, b_at(p)], raw_bc.at[mine, 0:N]), (x.at[:, c_at(p)], raw_bc.at[mine, N : 2 * N])]

    def pieces(q):
        out = []
        for d in (2, 1, 3):
            p = lax.rem(g + d, GROUPS)
            out.append(pltpu.make_async_remote_copy(
                x.at[:, lanes(p * chunks + q, WIDTH)], raw.at[q, mine], xsend.at[d, q],
                xrecv.at[d, q], device_id=peer(d)))
        out.append(pltpu.make_async_copy(
            x.at[:, lanes(g * chunks + q, WIDTH)], raw.at[q, mine], xown.at[q]))
        return out

    state_copies, step_copies, param_copies, local_copies = [], [], [], []
    for d in (2, 1, 3):
        p = lax.rem(g + d, GROUPS)
        for k, (src, dst) in enumerate(states(p)):
            state_copies.append(pltpu.make_async_remote_copy(
                src, dst, bsend.at[d, k], brecv.at[d, k], device_id=peer(d)))
        step_copies.append(pltpu.make_async_remote_copy(
            dt_packs.at[p], dts.at[g], bsend.at[d, 2], brecv.at[d, 2], device_id=peer(d)))
    for d in range(1, nf):
        for k, (src, dst) in enumerate(params):
            param_copies.append(pltpu.make_async_remote_copy(
                src, dst, psend.at[d, k], precv.at[d, k], device_id=sibling(d)))
    for k, (src, dst) in enumerate(states(g) + params):
        local_copies.append(pltpu.make_async_copy(src, dst, own_sem.at[k]))

    early = min(2, chunks)
    for copy in state_copies:
        copy.start()
    for copy in pieces(0):
        copy.start()
    @pl.when(z > 0)
    def _():
        pl.semaphore_signal(chain_ready, inc=1, device_id=along(f, z - 1))
        pl.semaphore_signal(plane_ready, inc=1, device_id=device(seg - 1, GROUPS - 1, nz))

    for copy in param_copies + local_copies:
        copy.start()

    steps_in.wait()
    part = rows // GROUPS
    slot = lax.broadcasted_iota(jnp.int32, (part, heads), 1) // (heads // GROUPS)
    blocks = [dt_own[k * part : (k + 1) * part, :].astype(F32) for k in range(GROUPS)]
    for p in range(GROUPS):
        packed = jnp.zeros((part, heads), F32)
        for k in range(GROUPS):
            turned = pltpu.roll(blocks[k], (k - p) % GROUPS * (heads // GROUPS), 1)
            packed = jnp.where(slot == k, turned, packed)
        dt_packs[p] = packed.astype(BF16)
    for copy in step_copies:
        copy.start()
    dts[g] = dt_packs[g]

    for q in range(1, early):
        for copy in pieces(q):
            copy.start()

    @pl.when(sends_halo)
    def _():
        packing[...] = jnp.zeros_like(packing)
        tail_copy().wait()
        for p in range(GROUPS):
            starts = [p * gw + k * WIDTH for k in range(chunks)]
            for k, at in enumerate(starts):
                packing[3 * k : 3 * k + 3, :] = tail[:, at : at + WIDTH].astype(F32)[HALO - 3 :]
            for k, at in enumerate((di + p * N, di + (GROUPS + p) * N)):
                packing[3 * chunks : 3 * chunks + 3, k * N : (k + 1) * N] = (
                    tail[:, at : at + N].astype(F32)[HALO - 3 :])
            packs[p] = packing[...].astype(BF16)

        @pl.when(tells_plane)
        def _():
            pl.semaphore_wait(plane_ready, GROUPS)

        for copy in halo_copies():
            copy.start()

    @pl.loop(early, chunks)
    def _(q):
        for copy in pieces(q):
            copy.start()

    @pl.when(z == 0)
    def _():
        a_buf[...] = jnp.zeros_like(a_buf)

    @pl.when(f == 0)
    def _():
        h_buf[...] = jnp.zeros_like(h_buf)

    @pl.when(z == 0)
    def _():
        decays[...] = jnp.ones_like(decays)

    fill_selection(sel)
    squares[...] = jnp.zeros_like(squares)
    halos[...] = jnp.zeros_like(halos)
    for copy in state_copies + step_copies + param_copies + local_copies:
        copy.wait()

    @pl.when(seg > 0)
    def _():
        halo_copies()[0].wait_recv()
        for k in range(chunks + 1):
            halos[k, 5:8, :] = halo[...].astype(F32)[3 * k : 3 * k + 3]

    per_bias = own // 128

    def bias_of(i):
        return biases[i // per_bias, pl.ds(lax.rem(i, per_bias), 1), :]

    ext[0:8, :] = halos[chunks]
    ext[8:, :] = raw_bc[...].astype(F32)
    keys[...] = silu_conv(ext, 0, taps, bias_of(di // N + g), b_at(g), N)
    queries = silu_conv(ext, N, taps, bias_of(di // N + GROUPS + g), c_at(g), N)
    to_front = lax.rem(GROUPS - g, GROUPS) * (heads // GROUPS)
    step_bias, rate_log, direct = (
        pltpu.roll(jnp.broadcast_to(jnp.concatenate([vectors[k, i] for i in range(nf)], axis=1), (8, heads)),
                   to_front, 1)[0:1] for k in range(3))
    lower = (lax.broadcasted_iota(jnp.int32, (rows, rows), 0)
             >= lax.broadcasted_iota(jnp.int32, (rows, rows), 1))
    ones = jnp.where(lower, 1.0, 0.0)
    scale = jnp.exp(rate_log)
    decayed = jnp.ones((1, heads), F32)
    for j in range(GROUPS):
        at = pl.ds(j * rows, rows)
        steps_of = dts[j].astype(F32)
        delta = jnp.concatenate(
            [pltpu.roll(steps_of, (GROUPS - k) % GROUPS * (heads // GROUPS), 1) for k in range(GROUPS)],
            axis=0) + step_bias
        delta = jnp.maximum(delta, 0.0) + jnp.log1p(jnp.exp(-jnp.abs(delta)))
        cum = lax.dot_general(ones, -scale * delta, (((1,), (0,)), ((), ())),
                              precision=lax.Precision.HIGHEST, preferred_element_type=F32)
        decay = jnp.exp(cum)
        source[j] = hi_lo(delta * jnp.exp(-cum))
        decay_2[j] = hi_lo(decay)
        carry_2[j] = hi_lo(decay * decayed)
        block_decay = decay[rows - 1 : rows, :]
        decayed = decayed * block_decay
        vec_2[j] = hi_lo(jnp.concatenate(
            [direct, block_decay, decayed, jnp.zeros((5, heads), F32)], axis=0))
        mine_q = queries[j * rows : (j + 1) * rows]
        scores = jnp.where(lower, dot(mine_q, keys[at, :], ((1,), (1,))), 0.0).astype(BF16)
        left[j] = jnp.concatenate([scores, mine_q], axis=1)
    my_decay[...] = jnp.broadcast_to(decayed, (8, heads))

    def decay_hop():
        return pltpu.make_async_remote_copy(
            next_decay, decays, dsend.at[0], drecv.at[0], device_id=along(f, z + 1))

    def local_step(q):
        for copy in pieces(q)[:3]:
            copy.wait_recv()
        pieces(q)[3].wait()
        here = lanes(q, WIDTH)
        ext[0:8, :] = halos[q]
        ext[8:, :] = raw[q].astype(F32)
        i = g * chunks + q
        bias = jnp.concatenate([bias_of(2 * i), bias_of(2 * i + 1)], axis=1)
        act = silu_conv(ext, 0, taps, bias, lanes(i, WIDTH), WIDTH)
        pick = sel[:, here]
        state = jnp.zeros((N, WIDTH), F32)
        for j in range(GROUPS):
            values = act[j * rows : (j + 1) * rows].astype(F32)
            weighted = (values * dot(source[j], pick)).astype(BF16)
            vec = dot(vec_2[j], pick)
            inner = dot(left[j], jnp.concatenate([weighted, state.astype(BF16)], axis=0))
            z_buf[q, j] = dot(decay_2[j], pick) * inner + vec[0:1, :] * values
            state = vec[1:2, :] * (state + dot(keys[pl.ds(j * rows, rows), :], weighted, ((0,), (0,))))
        p_buf[q] = state

    def hop(q):
        return pltpu.make_async_remote_copy(
            a_out.at[q], a_buf.at[q], csend.at[q], crecv.at[q], device_id=along(f, z + 1))

    def half(q, k):
        return pltpu.make_async_remote_copy(
            h_out.at[q], h_buf.at[q], hsend.at[k, q], hrecv.at[q], device_id=along(f + 1, k))

    def back(d, q):
        return pltpu.make_async_remote_copy(
            y_out.at[lax.rem(g + d, GROUPS), q], y_ref.at[:, lanes(g * chunks + q, WIDTH)],
            osend.at[d, q], orecv.at[d, q], device_id=peer(d))

    def through(pick):
        return dot(vec_2[GROUPS - 1], pick)[2:3, :]

    def chain_step(q):
        @pl.when(z > 0)
        def _():
            hop(q).wait_recv()

        @pl.when(z < nz - 1)
        def _():
            pick = sel[:, lanes(q, WIDTH)]
            a_out[q] = (p_buf[q] + through(pick) * a_buf[q].astype(F32)).astype(a_out.dtype)
            hop(q).start()

    def carry_step(q):
        pick = sel[:, lanes(q, WIDTH)]

        @pl.when(f > 0)
        def _():
            half(q, 0).wait_recv()

        state = a_buf[q].astype(F32) + dot(before_2[...], pick)[0:1, :] * h_buf[q].astype(F32)

        @pl.when(sends_half)
        def _():
            h_out[q] = (p_buf[q] + through(pick) * state).astype(h_out.dtype)
            for k in range(nz):
                half(q, k).start()

        low = state.astype(BF16)
        for j in range(GROUPS):
            carried = dot(left[j, :, N:], low) * dot(carry_2[j], pick)
            y_out[j, q] = (z_buf[q, j] + carried).astype(BF16)
        for d in range(1, GROUPS):
            back(d, q).start()
        y_ref[:, lanes(g * chunks + q, WIDTH)] = y_out[g, q]

    def bounded(v):
        return jnp.where(v < chunks, v, chunks)

    chain_lag = bounded(z)
    carry_lag = bounded(jnp.where(f == 0, z, nz - 1 + f))
    steps = chunks + min(chunks, nz - 1 + nf - 1)

    @pl.loop(0, steps)
    def _(i):
        @pl.when(i < chunks)
        def _():
            local_step(i)

        @pl.when(i == chain_lag)
        def _():
            @pl.when(z > 0)
            def _():
                decay_hop().wait_recv()

            before_2[...] = hi_lo(decays[...])

            @pl.when(z < nz - 1)
            def _():
                pl.semaphore_wait(chain_ready, 1)
                next_decay[...] = decays[...] * my_decay[...]
                decay_hop().start()

        @pl.when(jnp.logical_and(i >= chain_lag, i < chain_lag + chunks))
        def _():
            chain_step(i - chain_lag)

        @pl.when(jnp.logical_and(i >= carry_lag, i < carry_lag + chunks))
        def _():
            carry_step(i - carry_lag)

    @pl.loop(0, chunks)
    def _(q):
        for copy in pieces(q)[:3]:
            copy.wait_send()

    @pl.when(z < nz - 1)
    def _():
        decay_hop().wait_send()

        @pl.loop(0, chunks)
        def _(q):
            hop(q).wait_send()

    @pl.when(sends_half)
    def _():
        @pl.loop(0, chunks)
        def _(q):
            for k in range(nz):
                half(q, k).wait_send()

    @pl.when(sends_halo)
    def _():
        for copy in halo_copies():
            copy.wait_send()

    @pl.loop(0, chunks)
    def _(q):
        for d in range(1, GROUPS):
            back(d, q).wait_recv()
        for p in range(GROUPS):
            y = y_ref[:, lanes(p * chunks + q, WIDTH)].astype(F32)
            squares[p] = squares[p] + y * y
        for d in range(1, GROUPS):
            back(d, q).wait_send()

    for p in range(GROUPS):
        norm = lax.rsqrt(jnp.sum(squares[p], axis=1, keepdims=True) * (1.0 / gw) + 1e-05)
        scale_ref[:, p * 128 : (p + 1) * 128] = jnp.broadcast_to(norm, (rows, 128))


def mixer(x, dt, taps, bias, step, rate, skip, gain):
    rows, ch = x.shape
    heads = dt.shape[1]
    nf = lax.axis_size("fsdp")
    nz = lax.axis_size("ctx") // GROUPS
    gw = heads * P_SIZE // GROUPS
    chunks = gw // WIDTH
    length = rows * GROUPS
    packed_rows = -(-3 * (chunks + 1) // 16) * 16
    link = BF16 if nf * nz <= 8 else F32
    vm, dma = pltpu.VMEM, pltpu.SemaphoreType.DMA
    return pl.pallas_call(
        mixer_kernel,
        out_shape=(jax.ShapeDtypeStruct((rows, gw * GROUPS), BF16),
                   jax.ShapeDtypeStruct((rows, GROUPS * 128), F32),
                   jax.ShapeDtypeStruct((nf,) + gain.shape, F32)),
        in_specs=[HBM] * 8,
        out_specs=(WHOLE,) * 3,
        scratch_shapes=[
            vm((chunks, length, WIDTH), BF16),
            vm((length, 2 * N), BF16),
            vm((rows, heads), BF16),
            vm((GROUPS, rows // GROUPS, heads), BF16),
            vm((GROUPS, rows // GROUPS, heads), BF16),
            vm((HALO, ch), BF16),
            vm((packed_rows, WIDTH), F32),
            vm((GROUPS, packed_rows, WIDTH), BF16),
            vm((packed_rows, WIDTH), BF16),
            vm((chunks + 1, 8, WIDTH), F32),
            vm((4, ch), F32),
            vm((nf,) + bias.shape, F32),
            vm((3, nf) + step.shape, F32),
            vm((2 * heads, gw), BF16),
            vm((8 + length, WIDTH), F32),
            vm((length, N), BF16),
            vm((GROUPS, rows, 2 * N), BF16),
            vm((GROUPS, rows, 2 * heads), BF16),
            vm((GROUPS, rows, 2 * heads), BF16),
            vm((GROUPS, rows, 2 * heads), BF16),
            vm((GROUPS, 8, 2 * heads), BF16),
            vm((8, heads), F32),
            vm((8, heads), F32),
            vm((8, heads), F32),
            vm((8, 2 * heads), BF16),
            vm((chunks, GROUPS, rows, WIDTH), F32),
            vm((chunks, N, WIDTH), F32),
            vm((chunks, N, WIDTH), link),
            vm((chunks, N, WIDTH), link),
            vm((chunks, N, WIDTH), link),
            vm((chunks, N, WIDTH), link),
            vm((GROUPS, chunks, rows, WIDTH), BF16),
            vm((GROUPS, rows, WIDTH), F32),
            dma((GROUPS, chunks)), dma((GROUPS, chunks)), dma((GROUPS, 3)), dma((GROUPS, 3)),
            dma((nf, 6)), dma((nf, 6)), dma((GROUPS,)), dma((1,)), dma((1,)), dma((1,)),
            dma((chunks,)), dma((chunks,)), dma((nz, chunks)), dma((chunks,)),
            dma((GROUPS, chunks)), dma((GROUPS, chunks)), dma((chunks,)), dma((11,)), pltpu.SemaphoreType.REGULAR, pltpu.SemaphoreType.REGULAR,
        ],
        compiler_params=pltpu.CompilerParams(
            collective_id=0, has_side_effects=True, vmem_limit_bytes=51 << 20),
        name="mixer",
    )(x, dt, taps, bias, step, rate, skip, gain)


def norm_kernel(y, scale, gain, out, buf, sem):
    gw = y.shape[1] // GROUPS
    own = gain.shape[2]
    copies = []
    for p in range(GROUPS):
        factor = scale[:, p * 128 : (p + 1) * 128]
        for at in range(p * gw, (p + 1) * gw, 128):
            gains = gain[at // own, :, at % own : at % own + 128]
            buf[:, at : at + 128] = (y[:, at : at + 128].astype(F32) * factor * gains).astype(BF16)
        here = slice(p * gw, (p + 1) * gw)
        copies.append(pltpu.make_async_copy(buf.at[:, here], out.at[:, here], sem.at[p]))
        copies[-1].start()
    for copy in copies:
        copy.wait()


def norm(y, scale, gain):
    return pl.pallas_call(
        norm_kernel,
        out_shape=jax.ShapeDtypeStruct(y.shape, BF16),
        in_specs=[WHOLE] * 3,
        out_specs=HBM,
        scratch_shapes=[pltpu.VMEM(y.shape, BF16), pltpu.SemaphoreType.DMA((GROUPS,))],
        compiler_params=pltpu.CompilerParams(vmem_limit_bytes=16 << 20),
        name="norm",
    )(y, scale, gain)


def local(xbc, dt, conv_weight, conv_bias, dt_bias, a_log, skip, norm_gain):
    y, scale, gain = mixer(*(pltpu.with_memory_space_constraint(v, pltpu.HBM) for v in (
        xbc, dt, conv_weight, conv_bias.reshape(-1, 128), dt_bias.reshape(1, -1), a_log.reshape(1, -1),
        skip.reshape(1, -1), norm_gain.reshape(1, -1))))
    return norm(y, scale, gain)


def solution(mesh):
    placed = (
        P(("fsdp", "ctx"), None),
        P(("fsdp", "ctx"), None),
        P(None, "fsdp"),
        P("fsdp"),
        P("fsdp"),
        P("fsdp"),
        P("fsdp"),
        P("fsdp"),
    )
    return jax.shard_map(
        local, mesh=mesh, in_specs=placed, out_specs=P(("fsdp", "ctx"), None), check_vma=False
    )
```

```python
import jax
import jax.numpy as jnp
from jax import lax
from jax.experimental import pallas as pl
from jax.experimental.pallas import tpu as pltpu
from jax.sharding import PartitionSpec as P

P_SIZE = 64
N = 128
GROUPS = 4
HALO = 16
WIDTH = 256
F32, BF16 = jnp.float32, jnp.bfloat16
HBM = pl.BlockSpec(memory_space=pltpu.HBM)
WHOLE = pl.BlockSpec(memory_space=pltpu.VMEM)


def place():
    f, c = lax.axis_index("fsdp"), lax.axis_index("ctx")
    nz = lax.axis_size("ctx") // GROUPS
    nf = lax.axis_size("fsdp")
    g, z = lax.rem(c, GROUPS), c // GROUPS
    return f, c, g, z, nz, nf, f * nz + z


def device(seg, g, nz):
    return {"fsdp": seg // nz, "ctx": lax.rem(seg, nz) * GROUPS + g}


def lanes(index, size):
    return pl.ds(pl.multiple_of(index * size, 128), size)


def hi_lo(v):
    hi = v.astype(BF16)
    return jnp.concatenate([hi, (v - hi.astype(F32)).astype(BF16)], axis=1)


def dot(a, b, dims=((1,), (0,))):
    return lax.dot_general(a, b, (dims, ((), ())), preferred_element_type=F32)


def fill_selection(sel):
    heads = sel.shape[0] // 2
    row = lax.broadcasted_iota(jnp.int32, sel.shape, 0)
    col = lax.broadcasted_iota(jnp.int32, sel.shape, 1)
    row = jnp.where(row >= heads, row - heads, row)
    sel[...] = jnp.where(row == col // P_SIZE, 1.0, 0.0).astype(BF16)


def take(ref, sem):
    pltpu.make_async_copy(ref, ref, sem).wait()


def silu_conv(ext, start, taps, bias, at, size):
    rows = ext.shape[0] - 8
    total = bias
    for k in range(4):
        total = total + taps[k : k + 1, at] * ext[5 + k : 5 + k + rows, start : start + size]
    return (total / (1.0 + jnp.exp(-total))).astype(BF16)


def mixer_kernel(x, dt, taps_in, bias_in, step_in, rate_in, skip_in, gain_in,
                 y_ref, scale_ref, gain_ref,
                 raw, raw_bc, dt_own, dt_packs, dts, tail, packing, packs, halo, halos, taps, biases, vectors, sel, ext, keys, left, source, decay_2,
                 carry_2, vec_2, my_decay, next_decay, decays, before_2, z_buf, p_buf, a_buf, a_out, h_buf, h_out,
                 y_out, squares,
                 xsend, xrecv, bsend, brecv, psend, precv, tsend, trecv, dsend, drecv, csend, crecv,
                 hsend, hrecv, osend, orecv, own_sem, chain_ready, plane_ready):
    f, c, g, z, nz, nf, seg = place()
    last = nz * nf - 1
    rows = x.shape[0]
    chunks = raw.shape[0]
    gw = chunks * WIDTH
    di = gw * GROUPS
    heads = dt.shape[1]
    own = taps_in.shape[1]

    def peer(d):
        return {"fsdp": f, "ctx": z * GROUPS + lax.rem(g + d, GROUPS)}

    def sibling(d):
        return {"fsdp": lax.rem(f + d, nf), "ctx": c}

    def along(half, k):
        return {"fsdp": half, "ctx": k * GROUPS + g}

    def tail_copy():
        return pltpu.make_async_copy(x.at[pl.ds(rows - HALO, HALO), :], tail, own_sem.at[1])

    sends_halo = jnp.logical_and(g == GROUPS - 1, seg < last)
    sends_half = jnp.logical_and(z == nz - 1, f < nf - 1)
    tells_plane = jnp.logical_and(g == GROUPS - 1, z < nz - 1)

    barrier = pltpu.get_barrier_semaphore()
    for d in range(1, GROUPS):
        pl.semaphore_signal(barrier, inc=1, device_id=peer(d))
    for d in range(1, nf):
        pl.semaphore_signal(barrier, inc=1, device_id=sibling(d))

    @pl.when(z < nz - 1)
    def _():
        pl.semaphore_signal(barrier, inc=1, device_id=along(f, z + 1))

    @pl.when(tells_plane)
    def _():
        for p in range(GROUPS):
            pl.semaphore_signal(barrier, inc=1, device_id=device(seg + 1, p, nz))

    @pl.when(f > 0)
    def _():
        pl.semaphore_signal(barrier, inc=1, device_id=along(f - 1, nz - 1))

    @pl.when(jnp.logical_and(f > 0, z == 0))
    def _():
        pl.semaphore_signal(barrier, inc=1, device_id=device(seg - 1, GROUPS - 1, nz))

    steps_in = pltpu.make_async_copy(dt, dt_own, own_sem.at[0])
    steps_in.start()

    @pl.when(sends_halo)
    def _():
        tail_copy().start()

    more = jnp.where(z > 0, 2, 0) + jnp.where(sends_half, jnp.where(g == GROUPS - 1, nz + GROUPS, nz), 0)
    pl.semaphore_wait(barrier, GROUPS - 1 + nf - 1 + more)

    def b_at(p):
        return pl.ds(pl.multiple_of(di + p * N, 128), N)

    def c_at(p):
        return pl.ds(pl.multiple_of(di + (GROUPS + p) * N, 128), N)

    mine = pl.ds(pl.multiple_of(g * rows, 128), rows)

    def halo_copies():
        return [pltpu.make_async_remote_copy(
            packs.at[p], halo, tsend.at[0], trecv.at[0], device_id=device(seg + 1, p, nz))
            for p in range(GROUPS)]

    params = [(taps_in, taps.at[:, lanes(f, own)]), (bias_in, biases.at[f]), (step_in, vectors.at[0, f]),
              (rate_in, vectors.at[1, f]), (skip_in, vectors.at[2, f]), (gain_in, gain_ref.at[f])]

    def states(p):
        return [(x.at[:, b_at(p)], raw_bc.at[mine, 0:N]), (x.at[:, c_at(p)], raw_bc.at[mine, N : 2 * N])]

    def pieces(q):
        out = []
        for d in (2, 1, 3):
            p = lax.rem(g + d, GROUPS)
            out.append(pltpu.make_async_remote_copy(
                x.at[:, lanes(p * chunks + q, WIDTH)], raw.at[q, mine], xsend.at[0],
                xrecv.at[q], device_id=peer(d)))
        out.append(pltpu.make_async_copy(
            x.at[:, lanes(g * chunks + q, WIDTH)], raw.at[q, mine], xrecv.at[q]))
        return out

    state_copies, step_copies, param_copies, local_copies = [], [], [], []
    for d in (2, 1, 3):
        p = lax.rem(g + d, GROUPS)
        for k, (src, dst) in enumerate(states(p)):
            state_copies.append(pltpu.make_async_remote_copy(
                src, dst, bsend.at[0], brecv.at[0], device_id=peer(d)))
        step_copies.append(pltpu.make_async_remote_copy(
            dt_packs.at[p], dts.at[g], bsend.at[1], brecv.at[1], device_id=peer(d)))
    for d in range(1, nf):
        for k, (src, dst) in enumerate(params):
            param_copies.append(pltpu.make_async_remote_copy(
                src, dst, psend.at[k], precv.at[k], device_id=sibling(d)))
    for src, dst in states(g):
        local_copies.append(pltpu.make_async_copy(src, dst, brecv.at[0]))
    for k, (src, dst) in enumerate(params):
        local_copies.append(pltpu.make_async_copy(src, dst, precv.at[k]))

    early = min(2, chunks)
    for copy in state_copies:
        copy.start()
    for copy in pieces(0):
        copy.start()
    @pl.when(z > 0)
    def _():
        pl.semaphore_signal(chain_ready, inc=1, device_id=along(f, z - 1))
        pl.semaphore_signal(plane_ready, inc=1, device_id=device(seg - 1, GROUPS - 1, nz))

    for copy in param_copies + local_copies:
        copy.start()

    steps_in.wait()
    part = rows // GROUPS
    slot = lax.broadcasted_iota(jnp.int32, (part, heads), 1) // (heads // GROUPS)
    blocks = [dt_own[k * part : (k + 1) * part, :].astype(F32) for k in range(GROUPS)]
    for p in range(GROUPS):
        packed = jnp.zeros((part, heads), F32)
        for k in range(GROUPS):
            turned = pltpu.roll(blocks[k], (k - p) % GROUPS * (heads // GROUPS), 1)
            packed = jnp.where(slot == k, turned, packed)
        dt_packs[p] = packed.astype(BF16)
    for copy in step_copies:
        copy.start()
    dts[g] = dt_packs[g]

    for q in range(1, early):
        for copy in pieces(q):
            copy.start()

    @pl.when(sends_halo)
    def _():
        packing[...] = jnp.zeros_like(packing)
        tail_copy().wait()
        for p in range(GROUPS):
            starts = [p * gw + k * WIDTH for k in range(chunks)]
            for k, at in enumerate(starts):
                packing[3 * k : 3 * k + 3, :] = tail[:, at : at + WIDTH].astype(F32)[HALO - 3 :]
            for k, at in enumerate((di + p * N, di + (GROUPS + p) * N)):
                packing[3 * chunks : 3 * chunks + 3, k * N : (k + 1) * N] = (
                    tail[:, at : at + N].astype(F32)[HALO - 3 :])
            packs[p] = packing[...].astype(BF16)

        @pl.when(tells_plane)
        def _():
            pl.semaphore_wait(plane_ready, GROUPS)

        for copy in halo_copies():
            copy.start()

    @pl.loop(early, chunks)
    def _(q):
        for copy in pieces(q):
            copy.start()

    @pl.when(z == 0)
    def _():
        a_buf[...] = jnp.zeros_like(a_buf)

    @pl.when(f == 0)
    def _():
        h_buf[...] = jnp.zeros_like(h_buf)

    @pl.when(z == 0)
    def _():
        decays[...] = jnp.ones_like(decays)

    fill_selection(sel)
    squares[...] = jnp.zeros_like(squares)
    halos[...] = jnp.zeros_like(halos)
    take(raw_bc, brecv.at[0])
    take(dt_packs.at[0 : GROUPS - 1], brecv.at[1])
    take(taps, precv.at[0])
    take(biases, precv.at[1])
    for k in range(3):
        take(vectors.at[k], precv.at[2 + k])
    take(gain_ref, precv.at[5])

    @pl.when(seg > 0)
    def _():
        halo_copies()[0].wait_recv()
        for k in range(chunks + 1):
            halos[k, 5:8, :] = halo[...].astype(F32)[3 * k : 3 * k + 3]

    per_bias = own // 128

    def bias_of(i):
        return biases[i // per_bias, pl.ds(lax.rem(i, per_bias), 1), :]

    ext[0:8, :] = halos[chunks]
    ext[8:, :] = raw_bc[...].astype(F32)
    keys[...] = silu_conv(ext, 0, taps, bias_of(di // N + g), b_at(g), N)
    queries = silu_conv(ext, N, taps, bias_of(di // N + GROUPS + g), c_at(g), N)
    to_front = lax.rem(GROUPS - g, GROUPS) * (heads // GROUPS)
    step_bias, rate_log, direct = (
        pltpu.roll(jnp.broadcast_to(jnp.concatenate([vectors[k, i] for i in range(nf)], axis=1), (8, heads)),
                   to_front, 1)[0:1] for k in range(3))
    lower = (lax.broadcasted_iota(jnp.int32, (rows, rows), 0)
             >= lax.broadcasted_iota(jnp.int32, (rows, rows), 1))
    ones = jnp.where(lower, 1.0, 0.0)
    scale = jnp.exp(rate_log)
    decayed = jnp.ones((1, heads), F32)
    for j in range(GROUPS):
        at = pl.ds(j * rows, rows)
        steps_of = dts[j].astype(F32)
        delta = jnp.concatenate(
            [pltpu.roll(steps_of, (GROUPS - k) % GROUPS * (heads // GROUPS), 1) for k in range(GROUPS)],
            axis=0) + step_bias
        delta = jnp.maximum(delta, 0.0) + jnp.log1p(jnp.exp(-jnp.abs(delta)))
        cum = lax.dot_general(ones, -scale * delta, (((1,), (0,)), ((), ())),
                              precision=lax.Precision.HIGHEST, preferred_element_type=F32)
        decay = jnp.exp(cum)
        source[j] = hi_lo(delta * jnp.exp(-cum))
        decay_2[j] = hi_lo(decay)
        carry_2[j] = hi_lo(decay * decayed)
        block_decay = decay[rows - 1 : rows, :]
        decayed = decayed * block_decay
        vec_2[j] = hi_lo(jnp.concatenate(
            [direct, block_decay, decayed, jnp.zeros((5, heads), F32)], axis=0))
        mine_q = queries[j * rows : (j + 1) * rows]
        scores = jnp.where(lower, dot(mine_q, keys[at, :], ((1,), (1,))), 0.0).astype(BF16)
        left[j] = jnp.concatenate([scores, mine_q], axis=1)
    my_decay[...] = jnp.broadcast_to(decayed, (8, heads))

    def decay_hop():
        return pltpu.make_async_remote_copy(
            next_decay, decays, dsend.at[0], drecv.at[0], device_id=along(f, z + 1))

    def local_step(q):
        take(raw.at[q], xrecv.at[q])
        here = lanes(q, WIDTH)
        ext[0:8, :] = halos[q]
        ext[8:, :] = raw[q].astype(F32)
        i = g * chunks + q
        bias = jnp.concatenate([bias_of(2 * i), bias_of(2 * i + 1)], axis=1)
        act = silu_conv(ext, 0, taps, bias, lanes(i, WIDTH), WIDTH)
        pick = sel[:, here]
        state = jnp.zeros((N, WIDTH), F32)
        for j in range(GROUPS):
            values = act[j * rows : (j + 1) * rows].astype(F32)
            weighted = (values * dot(source[j], pick)).astype(BF16)
            vec = dot(vec_2[j], pick)
            inner = dot(left[j], jnp.concatenate([weighted, state.astype(BF16)], axis=0))
            z_buf[q, j] = dot(decay_2[j], pick) * inner + vec[0:1, :] * values
            state = vec[1:2, :] * (state + dot(keys[pl.ds(j * rows, rows), :], weighted, ((0,), (0,))))
        p_buf[q] = state

    def hop(q):
        return pltpu.make_async_remote_copy(
            a_out.at[q], a_buf.at[q], csend.at[0], crecv.at[q], device_id=along(f, z + 1))

    def half(q, k):
        return pltpu.make_async_remote_copy(
            h_out.at[q], h_buf.at[q], hsend.at[k], hrecv.at[q], device_id=along(f + 1, k))

    def back(d, q):
        return pltpu.make_async_remote_copy(
            y_out.at[lax.rem(g + d, GROUPS), q], y_ref.at[:, lanes(g * chunks + q, WIDTH)],
            osend.at[0], orecv.at[q], device_id=peer(d))

    def through(pick):
        return dot(vec_2[GROUPS - 1], pick)[2:3, :]

    def chain_step(q):
        @pl.when(z > 0)
        def _():
            hop(q).wait_recv()

        @pl.when(z < nz - 1)
        def _():
            pick = sel[:, lanes(q, WIDTH)]
            a_out[q] = (p_buf[q] + through(pick) * a_buf[q].astype(F32)).astype(a_out.dtype)
            hop(q).start()

    def carry_step(q):
        pick = sel[:, lanes(q, WIDTH)]

        @pl.when(f > 0)
        def _():
            half(q, 0).wait_recv()

        state = a_buf[q].astype(F32) + dot(before_2[...], pick)[0:1, :] * h_buf[q].astype(F32)

        @pl.when(sends_half)
        def _():
            h_out[q] = (p_buf[q] + through(pick) * state).astype(h_out.dtype)
            for k in range(nz):
                half(q, k).start()

        low = state.astype(BF16)
        for j in range(GROUPS):
            carried = dot(left[j, :, N:], low) * dot(carry_2[j], pick)
            y_out[j, q] = (z_buf[q, j] + carried).astype(BF16)
        for d in range(1, GROUPS):
            back(d, q).start()
        y_ref[:, lanes(g * chunks + q, WIDTH)] = y_out[g, q]

    def bounded(v):
        return jnp.where(v < chunks, v, chunks)

    chain_lag = bounded(z)
    carry_lag = bounded(jnp.where(f == 0, z, nz - 1 + f))
    steps = chunks + min(chunks, nz - 1 + nf - 1)

    @pl.loop(0, steps)
    def _(i):
        @pl.when(i < chunks)
        def _():
            local_step(i)

        @pl.when(i == chain_lag)
        def _():
            @pl.when(z > 0)
            def _():
                decay_hop().wait_recv()

            before_2[...] = hi_lo(decays[...])

            @pl.when(z < nz - 1)
            def _():
                pl.semaphore_wait(chain_ready, 1)
                next_decay[...] = decays[...] * my_decay[...]
                decay_hop().start()

        @pl.when(jnp.logical_and(i >= chain_lag, i < chain_lag + chunks))
        def _():
            chain_step(i - chain_lag)

        @pl.when(jnp.logical_and(i >= carry_lag, i < carry_lag + chunks))
        def _():
            carry_step(i - carry_lag)

    others = (GROUPS - 1) * rows
    take(raw.at[:, 0:others], xsend.at[0])
    take(raw_bc.at[0:others], bsend.at[0])
    take(dt_packs.at[0 : GROUPS - 1], bsend.at[1])
    take(taps.at[:, 0 : (nf - 1) * own], psend.at[0])
    take(biases.at[0 : nf - 1], psend.at[1])
    for k in range(3):
        take(vectors.at[k, 0 : nf - 1], psend.at[2 + k])
    take(gain_ref.at[0 : nf - 1], psend.at[5])

    @pl.when(z < nz - 1)
    def _():
        decay_hop().wait_send()

        take(a_out, csend.at[0])

    @pl.when(sends_half)
    def _():
        for k in range(nz):
            take(h_out, hsend.at[k])

    @pl.when(sends_halo)
    def _():
        take(packs, tsend.at[0])

    @pl.loop(0, chunks)
    def _(q):
        take(y_out.at[0 : GROUPS - 1, q], orecv.at[q])
        for p in range(GROUPS):
            y = y_ref[:, lanes(p * chunks + q, WIDTH)].astype(F32)
            squares[p] = squares[p] + y * y

    take(y_out.at[0 : GROUPS - 1], osend.at[0])

    for p in range(GROUPS):
        norm = lax.rsqrt(jnp.sum(squares[p], axis=1, keepdims=True) * (1.0 / gw) + 1e-05)
        scale_ref[:, p * 128 : (p + 1) * 128] = jnp.broadcast_to(norm, (rows, 128))


def mixer(x, dt, taps, bias, step, rate, skip, gain):
    rows, ch = x.shape
    heads = dt.shape[1]
    nf = lax.axis_size("fsdp")
    nz = lax.axis_size("ctx") // GROUPS
    gw = heads * P_SIZE // GROUPS
    chunks = gw // WIDTH
    length = rows * GROUPS
    packed_rows = -(-3 * (chunks + 1) // 16) * 16
    link = BF16 if nf * nz <= 8 else F32
    vm, dma = pltpu.VMEM, pltpu.SemaphoreType.DMA
    return pl.pallas_call(
        mixer_kernel,
        out_shape=(jax.ShapeDtypeStruct((rows, gw * GROUPS), BF16),
                   jax.ShapeDtypeStruct((rows, GROUPS * 128), F32),
                   jax.ShapeDtypeStruct((nf,) + gain.shape, F32)),
        in_specs=[HBM] * 8,
        out_specs=(WHOLE,) * 3,
        scratch_shapes=[
            vm((chunks, length, WIDTH), BF16),
            vm((length, 2 * N), BF16),
            vm((rows, heads), BF16),
            vm((GROUPS, rows // GROUPS, heads), BF16),
            vm((GROUPS, rows // GROUPS, heads), BF16),
            vm((HALO, ch), BF16),
            vm((packed_rows, WIDTH), F32),
            vm((GROUPS, packed_rows, WIDTH), BF16),
            vm((packed_rows, WIDTH), BF16),
            vm((chunks + 1, 8, WIDTH), F32),
            vm((4, ch), F32),
            vm((nf,) + bias.shape, F32),
            vm((3, nf) + step.shape, F32),
            vm((2 * heads, gw), BF16),
            vm((8 + length, WIDTH), F32),
            vm((length, N), BF16),
            vm((GROUPS, rows, 2 * N), BF16),
            vm((GROUPS, rows, 2 * heads), BF16),
            vm((GROUPS, rows, 2 * heads), BF16),
            vm((GROUPS, rows, 2 * heads), BF16),
            vm((GROUPS, 8, 2 * heads), BF16),
            vm((8, heads), F32),
            vm((8, heads), F32),
            vm((8, heads), F32),
            vm((8, 2 * heads), BF16),
            vm((chunks, GROUPS, rows, WIDTH), F32),
            vm((chunks, N, WIDTH), F32),
            vm((chunks, N, WIDTH), link),
            vm((chunks, N, WIDTH), link),
            vm((chunks, N, WIDTH), link),
            vm((chunks, N, WIDTH), link),
            vm((GROUPS, chunks, rows, WIDTH), BF16),
            vm((GROUPS, rows, WIDTH), F32),
            dma((1,)), dma((chunks,)), dma((2,)), dma((2,)), dma((6,)), dma((6,)), dma((1,)), dma((1,)),
            dma((1,)), dma((1,)), dma((1,)), dma((chunks,)), dma((nz,)), dma((chunks,)),
            dma((1,)), dma((chunks,)), dma((2,)), pltpu.SemaphoreType.REGULAR, pltpu.SemaphoreType.REGULAR,
        ],
        compiler_params=pltpu.CompilerParams(
            collective_id=0, has_side_effects=True, vmem_limit_bytes=51 << 20),
        name="mixer",
    )(x, dt, taps, bias, step, rate, skip, gain)


def norm_kernel(y, scale, gain, out, buf, sem):
    gw = y.shape[1] // GROUPS
    own = gain.shape[2]
    copies = []
    for p in range(GROUPS):
        factor = scale[:, p * 128 : (p + 1) * 128]
        for at in range(p * gw, (p + 1) * gw, 128):
            gains = gain[at // own, :, at % own : at % own + 128]
            buf[:, at : at + 128] = (y[:, at : at + 128].astype(F32) * factor * gains).astype(BF16)
        here = slice(p * gw, (p + 1) * gw)
        copies.append(pltpu.make_async_copy(buf.at[:, here], out.at[:, here], sem.at[p]))
        copies[-1].start()
    for copy in copies:
        copy.wait()


def norm(y, scale, gain):
    return pl.pallas_call(
        norm_kernel,
        out_shape=jax.ShapeDtypeStruct(y.shape, BF16),
        in_specs=[WHOLE] * 3,
        out_specs=HBM,
        scratch_shapes=[pltpu.VMEM(y.shape, BF16), pltpu.SemaphoreType.DMA((GROUPS,))],
        compiler_params=pltpu.CompilerParams(vmem_limit_bytes=16 << 20),
        name="norm",
    )(y, scale, gain)


def local(xbc, dt, conv_weight, conv_bias, dt_bias, a_log, skip, norm_gain):
    y, scale, gain = mixer(*(pltpu.with_memory_space_constraint(v, pltpu.HBM) for v in (
        xbc, dt, conv_weight, conv_bias.reshape(-1, 128), dt_bias.reshape(1, -1), a_log.reshape(1, -1),
        skip.reshape(1, -1), norm_gain.reshape(1, -1))))
    return norm(y, scale, gain)


def solution(mesh):
    placed = (
        P(("fsdp", "ctx"), None),
        P(("fsdp", "ctx"), None),
        P(None, "fsdp"),
        P("fsdp"),
        P("fsdp"),
        P("fsdp"),
        P("fsdp"),
        P("fsdp"),
    )
    return jax.shard_map(
        local, mesh=mesh, in_specs=placed, out_specs=P(("fsdp", "ctx"), None), check_vma=False
    )
```

```python
import jax
import jax.numpy as jnp
from jax import lax
from jax.experimental import pallas as pl
from jax.experimental.pallas import tpu as pltpu
from jax.sharding import PartitionSpec as P

P_SIZE = 64
N = 128
GROUPS = 4
HALO = 16
WIDTH = 256
LATE = 2
F32, BF16 = jnp.float32, jnp.bfloat16
HBM = pl.BlockSpec(memory_space=pltpu.HBM)
WHOLE = pl.BlockSpec(memory_space=pltpu.VMEM)


def place():
    f, c = lax.axis_index("fsdp"), lax.axis_index("ctx")
    nz = lax.axis_size("ctx") // GROUPS
    nf = lax.axis_size("fsdp")
    g, z = lax.rem(c, GROUPS), c // GROUPS
    return f, c, g, z, nz, nf, f * nz + z


def device(seg, g, nz):
    return {"fsdp": seg // nz, "ctx": lax.rem(seg, nz) * GROUPS + g}


def lanes(index, size):
    return pl.ds(pl.multiple_of(index * size, 128), size)


def hi_lo(v):
    hi = v.astype(BF16)
    return jnp.concatenate([hi, (v - hi.astype(F32)).astype(BF16)], axis=1)


def dot(a, b, dims=((1,), (0,))):
    return lax.dot_general(a, b, (dims, ((), ())), preferred_element_type=F32)


def fill_selection(sel):
    heads = sel.shape[0] // 2
    row = lax.broadcasted_iota(jnp.int32, sel.shape, 0)
    col = lax.broadcasted_iota(jnp.int32, sel.shape, 1)
    row = jnp.where(row >= heads, row - heads, row)
    sel[...] = jnp.where(row == col // P_SIZE, 1.0, 0.0).astype(BF16)


def take(ref, sem):
    pltpu.make_async_copy(ref, ref, sem).wait()


def silu_conv(ext, start, taps, bias, at, size):
    rows = ext.shape[0] - 8
    total = bias
    for k in range(4):
        total = total + taps[k : k + 1, at] * ext[5 + k : 5 + k + rows, start : start + size]
    return (total / (1.0 + jnp.exp(-total))).astype(BF16)


def mixer_kernel(x, dt, taps_in, bias_in, step_in, rate_in, skip_in, gain_in,
                 y_ref, scale_ref, gain_ref,
                 raw, raw_bc, dt_own, dt_packs, dts, tail, packing, packs, halo, halos, taps, biases, vectors, sel, ext, keys, left, source, decay_2,
                 carry_2, vec_2, my_decay, next_decay, decays, before_2, z_buf, p_buf, a_buf, a_out, h_buf, h_out,
                 y_out, squares,
                 xsend, xrecv, bsend, brecv, psend, precv, tsend, trecv, dsend, drecv, csend, crecv,
                 hsend, hrecv, osend, orecv, own_sem, chain_ready, plane_ready):
    f, c, g, z, nz, nf, seg = place()
    last = nz * nf - 1
    rows = x.shape[0]
    chunks = raw.shape[0]
    gw = chunks * WIDTH
    di = gw * GROUPS
    heads = dt.shape[1]
    own = taps_in.shape[1]

    def peer(d):
        return {"fsdp": f, "ctx": z * GROUPS + lax.rem(g + d, GROUPS)}

    def sibling(d):
        return {"fsdp": lax.rem(f + d, nf), "ctx": c}

    def along(half, k):
        return {"fsdp": half, "ctx": k * GROUPS + g}

    def tail_copy():
        return pltpu.make_async_copy(x.at[pl.ds(rows - HALO, HALO), :], tail, own_sem.at[1])

    sends_halo = jnp.logical_and(g == GROUPS - 1, seg < last)
    sends_half = jnp.logical_and(z == nz - 1, f < nf - 1)
    tells_plane = jnp.logical_and(g == GROUPS - 1, z < nz - 1)

    barrier = pltpu.get_barrier_semaphore()
    for d in range(1, GROUPS):
        pl.semaphore_signal(barrier, inc=1, device_id=peer(d))
    for d in range(1, nf):
        pl.semaphore_signal(barrier, inc=1, device_id=sibling(d))

    @pl.when(z < nz - 1)
    def _():
        pl.semaphore_signal(barrier, inc=1, device_id=along(f, z + 1))

    @pl.when(tells_plane)
    def _():
        for p in range(GROUPS):
            pl.semaphore_signal(barrier, inc=1, device_id=device(seg + 1, p, nz))

    @pl.when(f > 0)
    def _():
        pl.semaphore_signal(barrier, inc=1, device_id=along(f - 1, nz - 1))

    @pl.when(jnp.logical_and(f > 0, z == 0))
    def _():
        pl.semaphore_signal(barrier, inc=1, device_id=device(seg - 1, GROUPS - 1, nz))

    steps_in = pltpu.make_async_copy(dt, dt_own, own_sem.at[0])
    steps_in.start()

    @pl.when(sends_halo)
    def _():
        tail_copy().start()

    more = jnp.where(z > 0, 2, 0) + jnp.where(sends_half, jnp.where(g == GROUPS - 1, nz + GROUPS, nz), 0)
    pl.semaphore_wait(barrier, GROUPS - 1 + nf - 1 + more)

    def b_at(p):
        return pl.ds(pl.multiple_of(di + p * N, 128), N)

    def c_at(p):
        return pl.ds(pl.multiple_of(di + (GROUPS + p) * N, 128), N)

    mine = pl.ds(pl.multiple_of(g * rows, 128), rows)

    def halo_copies():
        return [pltpu.make_async_remote_copy(
            packs.at[p], halo, tsend.at[0], trecv.at[0], device_id=device(seg + 1, p, nz))
            for p in range(GROUPS)]

    params = [(taps_in, taps.at[:, lanes(f, own)]), (bias_in, biases.at[f]), (step_in, vectors.at[0, f]),
              (rate_in, vectors.at[1, f]), (skip_in, vectors.at[2, f]), (gain_in, gain_ref.at[f])]

    def states(p):
        return [(x.at[:, b_at(p)], raw_bc.at[mine, 0:N]), (x.at[:, c_at(p)], raw_bc.at[mine, N : 2 * N])]

    def pieces(q):
        out = []
        for d in (2, 1, 3):
            p = lax.rem(g + d, GROUPS)
            out.append(pltpu.make_async_remote_copy(
                x.at[:, lanes(p * chunks + q, WIDTH)], raw.at[q, mine], xsend.at[0],
                xrecv.at[q], device_id=peer(d)))
        out.append(pltpu.make_async_copy(
            x.at[:, lanes(g * chunks + q, WIDTH)], raw.at[q, mine], xrecv.at[q]))
        return out

    slots = (0, 1, 2, 2, 2, 3)
    state_copies, step_copies, param_copies, local_copies = [], [], [], []
    for d in (2, 1, 3):
        p = lax.rem(g + d, GROUPS)
        for k, (src, dst) in enumerate(states(p)):
            state_copies.append(pltpu.make_async_remote_copy(
                src, dst, bsend.at[0], brecv.at[0], device_id=peer(d)))
        step_copies.append(pltpu.make_async_remote_copy(
            dt_packs.at[p], dts.at[g], bsend.at[1], brecv.at[1], device_id=peer(d)))
    for d in range(1, nf):
        for k, (src, dst) in enumerate(params):
            param_copies.append(pltpu.make_async_remote_copy(
                src, dst, psend.at[slots[k]], precv.at[slots[k]], device_id=sibling(d)))
    for src, dst in states(g):
        local_copies.append(pltpu.make_async_copy(src, dst, brecv.at[0]))
    for k, (src, dst) in enumerate(params):
        local_copies.append(pltpu.make_async_copy(src, dst, precv.at[slots[k]]))

    early = min(2, chunks)
    for copy in state_copies:
        copy.start()
    for copy in pieces(0):
        copy.start()
    @pl.when(z > 0)
    def _():
        pl.semaphore_signal(chain_ready, inc=1, device_id=along(f, z - 1))
        pl.semaphore_signal(plane_ready, inc=1, device_id=device(seg - 1, GROUPS - 1, nz))

    for copy in param_copies + local_copies:
        copy.start()

    steps_in.wait()
    part = rows // GROUPS
    slot = lax.broadcasted_iota(jnp.int32, (part, heads), 1) // (heads // GROUPS)
    blocks = [dt_own[k * part : (k + 1) * part, :].astype(F32) for k in range(GROUPS)]
    for p in range(GROUPS):
        packed = jnp.zeros((part, heads), F32)
        for k in range(GROUPS):
            turned = pltpu.roll(blocks[k], (k - p) % GROUPS * (heads // GROUPS), 1)
            packed = jnp.where(slot == k, turned, packed)
        dt_packs[p] = packed.astype(BF16)
    for copy in step_copies:
        copy.start()
    dts[g] = dt_packs[g]

    for q in range(1, early):
        for copy in pieces(q):
            copy.start()

    @pl.when(sends_halo)
    def _():
        packing[...] = jnp.zeros_like(packing)
        tail_copy().wait()
        for p in range(GROUPS):
            starts = [p * gw + k * WIDTH for k in range(chunks)]
            for k, at in enumerate(starts):
                packing[3 * k : 3 * k + 3, :] = tail[:, at : at + WIDTH].astype(F32)[HALO - 3 :]
            for k, at in enumerate((di + p * N, di + (GROUPS + p) * N)):
                packing[3 * chunks : 3 * chunks + 3, k * N : (k + 1) * N] = (
                    tail[:, at : at + N].astype(F32)[HALO - 3 :])
            packs[p] = packing[...].astype(BF16)

        @pl.when(tells_plane)
        def _():
            pl.semaphore_wait(plane_ready, GROUPS)

        for copy in halo_copies():
            copy.start()

    @pl.loop(early, chunks)
    def _(q):
        for copy in pieces(q):
            copy.start()

    @pl.when(z == 0)
    def _():
        a_buf[...] = jnp.zeros_like(a_buf)

    @pl.when(f == 0)
    def _():
        h_buf[...] = jnp.zeros_like(h_buf)

    @pl.when(z == 0)
    def _():
        decays[...] = jnp.ones_like(decays)

    fill_selection(sel)
    squares[...] = jnp.zeros_like(squares)
    halos[...] = jnp.zeros_like(halos)
    take(raw_bc, brecv.at[0])
    take(dt_packs.at[0 : GROUPS - 1], brecv.at[1])
    take(taps, precv.at[0])
    take(biases, precv.at[1])
    take(vectors, precv.at[2])
    take(gain_ref, precv.at[3])

    @pl.when(seg > 0)
    def _():
        halo_copies()[0].wait_recv()
        for k in range(chunks + 1):
            halos[k, 5:8, :] = halo[...].astype(F32)[3 * k : 3 * k + 3]

    per_bias = own // 128

    def bias_of(i):
        return biases[i // per_bias, pl.ds(lax.rem(i, per_bias), 1), :]

    ext[0:8, :] = halos[chunks]
    ext[8:, :] = raw_bc[...].astype(F32)
    keys[...] = silu_conv(ext, 0, taps, bias_of(di // N + g), b_at(g), N)
    queries = silu_conv(ext, N, taps, bias_of(di // N + GROUPS + g), c_at(g), N)
    to_front = lax.rem(GROUPS - g, GROUPS) * (heads // GROUPS)
    step_bias, rate_log, direct = (
        pltpu.roll(jnp.broadcast_to(jnp.concatenate([vectors[k, i] for i in range(nf)], axis=1), (8, heads)),
                   to_front, 1)[0:1] for k in range(3))
    lower = (lax.broadcasted_iota(jnp.int32, (rows, rows), 0)
             >= lax.broadcasted_iota(jnp.int32, (rows, rows), 1))
    ones = jnp.where(lower, 1.0, 0.0)
    scale = jnp.exp(rate_log)
    decayed = jnp.ones((1, heads), F32)
    for j in range(GROUPS):
        at = pl.ds(j * rows, rows)
        steps_of = dts[j].astype(F32)
        delta = jnp.concatenate(
            [pltpu.roll(steps_of, (GROUPS - k) % GROUPS * (heads // GROUPS), 1) for k in range(GROUPS)],
            axis=0) + step_bias
        delta = jnp.maximum(delta, 0.0) + jnp.log1p(jnp.exp(-jnp.abs(delta)))
        cum = lax.dot_general(ones, -scale * delta, (((1,), (0,)), ((), ())),
                              precision=lax.Precision.HIGHEST, preferred_element_type=F32)
        decay = jnp.exp(cum)
        source[j] = hi_lo(delta * jnp.exp(-cum))
        decay_2[j] = hi_lo(decay)
        carry_2[j] = hi_lo(decay * decayed)
        block_decay = decay[rows - 1 : rows, :]
        decayed = decayed * block_decay
        vec_2[j] = hi_lo(jnp.concatenate(
            [direct, block_decay, decayed, jnp.zeros((5, heads), F32)], axis=0))
        mine_q = queries[j * rows : (j + 1) * rows]
        scores = jnp.where(lower, dot(mine_q, keys[at, :], ((1,), (1,))), 0.0).astype(BF16)
        left[j] = jnp.concatenate([scores, mine_q], axis=1)
    my_decay[...] = jnp.broadcast_to(decayed, (8, heads))

    def decay_hop():
        return pltpu.make_async_remote_copy(
            next_decay, decays, dsend.at[0], drecv.at[0], device_id=along(f, z + 1))

    def local_step(q):
        take(raw.at[q], xrecv.at[q])
        here = lanes(q, WIDTH)
        ext[0:8, :] = halos[q]
        ext[8:, :] = raw[q].astype(F32)
        i = g * chunks + q
        bias = jnp.concatenate([bias_of(2 * i), bias_of(2 * i + 1)], axis=1)
        act = silu_conv(ext, 0, taps, bias, lanes(i, WIDTH), WIDTH)
        pick = sel[:, here]
        state = jnp.zeros((N, WIDTH), F32)
        for j in range(GROUPS):
            values = act[j * rows : (j + 1) * rows].astype(F32)
            weighted = (values * dot(source[j], pick)).astype(BF16)
            vec = dot(vec_2[j], pick)
            inner = dot(left[j], jnp.concatenate([weighted, state.astype(BF16)], axis=0))
            z_buf[q, j] = dot(decay_2[j], pick) * inner + vec[0:1, :] * values
            state = vec[1:2, :] * (state + dot(keys[pl.ds(j * rows, rows), :], weighted, ((0,), (0,))))
        p_buf[q] = state

    def hop(q):
        return pltpu.make_async_remote_copy(
            a_out.at[q], a_buf.at[q], csend.at[0], crecv.at[q], device_id=along(f, z + 1))

    def half(q, k):
        return pltpu.make_async_remote_copy(
            h_out.at[q], h_buf.at[q], hsend.at[k], hrecv.at[q], device_id=along(f + 1, k))

    def back(d, q):
        return pltpu.make_async_remote_copy(
            y_out.at[lax.rem(g + d, GROUPS), q], y_ref.at[:, lanes(g * chunks + q, WIDTH)],
            osend.at[0], orecv.at[jnp.maximum(q - chunks + LATE + 1, 0)], device_id=peer(d))

    def through(pick):
        return dot(vec_2[GROUPS - 1], pick)[2:3, :]

    def chain_step(q):
        @pl.when(z > 0)
        def _():
            hop(q).wait_recv()

        @pl.when(z < nz - 1)
        def _():
            pick = sel[:, lanes(q, WIDTH)]
            a_out[q] = (p_buf[q] + through(pick) * a_buf[q].astype(F32)).astype(a_out.dtype)
            hop(q).start()

    def carry_step(q):
        pick = sel[:, lanes(q, WIDTH)]

        @pl.when(f > 0)
        def _():
            half(q, 0).wait_recv()

        state = a_buf[q].astype(F32) + dot(before_2[...], pick)[0:1, :] * h_buf[q].astype(F32)

        @pl.when(sends_half)
        def _():
            h_out[q] = (p_buf[q] + through(pick) * state).astype(h_out.dtype)
            for k in range(nz):
                half(q, k).start()

        low = state.astype(BF16)
        for j in range(GROUPS):
            carried = dot(left[j, :, N:], low) * dot(carry_2[j], pick)
            y_out[j, q] = (z_buf[q, j] + carried).astype(BF16)
        for d in range(1, GROUPS):
            back(d, q).start()
        y_ref[:, lanes(g * chunks + q, WIDTH)] = y_out[g, q]

    def bounded(v):
        return jnp.where(v < chunks, v, chunks)

    chain_lag = bounded(z)
    carry_lag = bounded(jnp.where(f == 0, z, nz - 1 + f))
    steps = chunks + min(chunks, nz - 1 + nf - 1)

    @pl.loop(0, steps)
    def _(i):
        @pl.when(i < chunks)
        def _():
            local_step(i)

        @pl.when(i == chain_lag)
        def _():
            @pl.when(z > 0)
            def _():
                decay_hop().wait_recv()

            before_2[...] = hi_lo(decays[...])

            @pl.when(z < nz - 1)
            def _():
                pl.semaphore_wait(chain_ready, 1)
                next_decay[...] = decays[...] * my_decay[...]
                decay_hop().start()

        @pl.when(jnp.logical_and(i >= chain_lag, i < chain_lag + chunks))
        def _():
            chain_step(i - chain_lag)

        @pl.when(jnp.logical_and(i >= carry_lag, i < carry_lag + chunks))
        def _():
            carry_step(i - carry_lag)

    others = (GROUPS - 1) * rows
    take(raw.at[:, 0:others], xsend.at[0])
    take(raw_bc.at[0:others], bsend.at[0])
    take(dt_packs.at[0 : GROUPS - 1], bsend.at[1])
    take(taps.at[:, 0 : (nf - 1) * own], psend.at[0])
    take(biases.at[0 : nf - 1], psend.at[1])
    take(vectors.at[:, 0 : nf - 1], psend.at[2])
    take(gain_ref.at[0 : nf - 1], psend.at[3])

    @pl.when(z < nz - 1)
    def _():
        decay_hop().wait_send()

        take(a_out, csend.at[0])

    @pl.when(sends_half)
    def _():
        for k in range(nz):
            take(h_out, hsend.at[k])

    @pl.when(sends_halo)
    def _():
        take(packs, tsend.at[0])

    def add_squares(q):
        for p in range(GROUPS):
            y = y_ref[:, lanes(p * chunks + q, WIDTH)].astype(F32)
            squares[p] = squares[p] + y * y

    take(y_out.at[0 : GROUPS - 1, 0 : chunks - LATE], orecv.at[0])
    pl.loop(0, chunks - LATE)(add_squares)

    @pl.loop(chunks - LATE, chunks)
    def _(q):
        take(y_out.at[0 : GROUPS - 1, q], orecv.at[q - chunks + LATE + 1])
        add_squares(q)

    take(y_out.at[0 : GROUPS - 1], osend.at[0])

    for p in range(GROUPS):
        norm = lax.rsqrt(jnp.sum(squares[p], axis=1, keepdims=True) * (1.0 / gw) + 1e-05)
        scale_ref[:, p * 128 : (p + 1) * 128] = jnp.broadcast_to(norm, (rows, 128))


def mixer(x, dt, taps, bias, step, rate, skip, gain):
    rows, ch = x.shape
    heads = dt.shape[1]
    nf = lax.axis_size("fsdp")
    nz = lax.axis_size("ctx") // GROUPS
    gw = heads * P_SIZE // GROUPS
    chunks = gw // WIDTH
    length = rows * GROUPS
    packed_rows = -(-3 * (chunks + 1) // 16) * 16
    link = BF16 if nf * nz <= 8 else F32
    vm, dma = pltpu.VMEM, pltpu.SemaphoreType.DMA
    return pl.pallas_call(
        mixer_kernel,
        out_shape=(jax.ShapeDtypeStruct((rows, gw * GROUPS), BF16),
                   jax.ShapeDtypeStruct((rows, GROUPS * 128), F32),
                   jax.ShapeDtypeStruct((nf,) + gain.shape, F32)),
        in_specs=[HBM] * 8,
        out_specs=(WHOLE,) * 3,
        scratch_shapes=[
            vm((chunks, length, WIDTH), BF16),
            vm((length, 2 * N), BF16),
            vm((rows, heads), BF16),
            vm((GROUPS, rows // GROUPS, heads), BF16),
            vm((GROUPS, rows // GROUPS, heads), BF16),
            vm((HALO, ch), BF16),
            vm((packed_rows, WIDTH), F32),
            vm((GROUPS, packed_rows, WIDTH), BF16),
            vm((packed_rows, WIDTH), BF16),
            vm((chunks + 1, 8, WIDTH), F32),
            vm((4, ch), F32),
            vm((nf,) + bias.shape, F32),
            vm((3, nf) + step.shape, F32),
            vm((2 * heads, gw), BF16),
            vm((8 + length, WIDTH), F32),
            vm((length, N), BF16),
            vm((GROUPS, rows, 2 * N), BF16),
            vm((GROUPS, rows, 2 * heads), BF16),
            vm((GROUPS, rows, 2 * heads), BF16),
            vm((GROUPS, rows, 2 * heads), BF16),
            vm((GROUPS, 8, 2 * heads), BF16),
            vm((8, heads), F32),
            vm((8, heads), F32),
            vm((8, heads), F32),
            vm((8, 2 * heads), BF16),
            vm((chunks, GROUPS, rows, WIDTH), F32),
            vm((chunks, N, WIDTH), F32),
            vm((chunks, N, WIDTH), link),
            vm((chunks, N, WIDTH), link),
            vm((chunks, N, WIDTH), link),
            vm((chunks, N, WIDTH), link),
            vm((GROUPS, chunks, rows, WIDTH), BF16),
            vm((GROUPS, rows, WIDTH), F32),
            dma((1,)), dma((chunks,)), dma((2,)), dma((2,)), dma((4,)), dma((4,)), dma((1,)), dma((1,)),
            dma((1,)), dma((1,)), dma((1,)), dma((chunks,)), dma((nz,)), dma((chunks,)),
            dma((1,)), dma((LATE + 1,)), dma((2,)), pltpu.SemaphoreType.REGULAR, pltpu.SemaphoreType.REGULAR,
        ],
        compiler_params=pltpu.CompilerParams(
            collective_id=0, has_side_effects=True, vmem_limit_bytes=51 << 20),
        name="mixer",
    )(x, dt, taps, bias, step, rate, skip, gain)


def norm_kernel(y, scale, gain, out, buf, sem):
    gw = y.shape[1] // GROUPS
    own = gain.shape[2]
    copies = []
    for p in range(GROUPS):
        factor = scale[:, p * 128 : (p + 1) * 128]
        for at in range(p * gw, (p + 1) * gw, 128):
            gains = gain[at // own, :, at % own : at % own + 128]
            buf[:, at : at + 128] = (y[:, at : at + 128].astype(F32) * factor * gains).astype(BF16)
        here = slice(p * gw, (p + 1) * gw)
        copies.append(pltpu.make_async_copy(buf.at[:, here], out.at[:, here], sem.at[p]))
        copies[-1].start()
    for copy in copies:
        copy.wait()


def norm(y, scale, gain):
    return pl.pallas_call(
        norm_kernel,
        out_shape=jax.ShapeDtypeStruct(y.shape, BF16),
        in_specs=[WHOLE] * 3,
        out_specs=HBM,
        scratch_shapes=[pltpu.VMEM(y.shape, BF16), pltpu.SemaphoreType.DMA((GROUPS,))],
        compiler_params=pltpu.CompilerParams(vmem_limit_bytes=16 << 20),
        name="norm",
    )(y, scale, gain)


def local(xbc, dt, conv_weight, conv_bias, dt_bias, a_log, skip, norm_gain):
    y, scale, gain = mixer(*(pltpu.with_memory_space_constraint(v, pltpu.HBM) for v in (
        xbc, dt, conv_weight, conv_bias.reshape(-1, 128), dt_bias.reshape(1, -1), a_log.reshape(1, -1),
        skip.reshape(1, -1), norm_gain.reshape(1, -1))))
    return norm(y, scale, gain)


def solution(mesh):
    placed = (
        P(("fsdp", "ctx"), None),
        P(("fsdp", "ctx"), None),
        P(None, "fsdp"),
        P("fsdp"),
        P("fsdp"),
        P("fsdp"),
        P("fsdp"),
        P("fsdp"),
    )
    return jax.shard_map(
        local, mesh=mesh, in_specs=placed, out_specs=P(("fsdp", "ctx"), None), check_vma=False
    )
```

```python
import jax
import jax.numpy as jnp
from jax import lax
from jax.experimental import pallas as pl
from jax.experimental.pallas import tpu as pltpu
from jax.sharding import PartitionSpec as P

P_SIZE = 64
N = 128
GROUPS = 4
HALO = 16
WIDTH = 256
LATE = 2
F32, BF16 = jnp.float32, jnp.bfloat16
HBM = pl.BlockSpec(memory_space=pltpu.HBM)
WHOLE = pl.BlockSpec(memory_space=pltpu.VMEM)


def place():
    f, c = lax.axis_index("fsdp"), lax.axis_index("ctx")
    nz = lax.axis_size("ctx") // GROUPS
    nf = lax.axis_size("fsdp")
    g, z = lax.rem(c, GROUPS), c // GROUPS
    return f, c, g, z, nz, nf, f * nz + z


def device(seg, g, nz):
    return {"fsdp": seg // nz, "ctx": lax.rem(seg, nz) * GROUPS + g}


def lanes(index, size):
    return pl.ds(pl.multiple_of(index * size, 128), size)


def hi_lo(v):
    hi = v.astype(BF16)
    return jnp.concatenate([hi, (v - hi.astype(F32)).astype(BF16)], axis=1)


def dot(a, b, dims=((1,), (0,))):
    return lax.dot_general(a, b, (dims, ((), ())), preferred_element_type=F32)


def fill_selection(sel):
    heads = sel.shape[0] // 2
    row = lax.broadcasted_iota(jnp.int32, sel.shape, 0)
    col = lax.broadcasted_iota(jnp.int32, sel.shape, 1)
    row = jnp.where(row >= heads, row - heads, row)
    sel[...] = jnp.where(row == col // P_SIZE, 1.0, 0.0).astype(BF16)


def take(ref, sem):
    pltpu.make_async_copy(ref, ref, sem).wait()


def silu_conv(ext, start, taps, bias, at, size):
    rows = ext.shape[0] - 8
    total = bias
    for k in range(4):
        total = total + taps[k : k + 1, at] * ext[5 + k : 5 + k + rows, start : start + size]
    return (total / (1.0 + jnp.exp(-total))).astype(BF16)


def mixer_kernel(x, dt, taps_in, bias_in, step_in, rate_in, skip_in, gain_in,
                 y_ref, scale_ref, gain_ref,
                 raw, raw_bc, dt_own, dt_packs, dts, tail, packing, packs, halo, halos, taps, biases, vectors, sel, ext, keys, left, source, decay_2,
                 carry_2, vec_2, my_decay, next_decay, decays, before_2, z_buf, p_buf, a_buf, a_out, h_buf, h_out,
                 y_out, squares,
                 xsend, xrecv, bsend, brecv, psend, precv, tsend, trecv, dsend, drecv, csend, crecv,
                 hsend, hrecv, osend, orecv, own_sem, chain_ready, plane_ready):
    f, c, g, z, nz, nf, seg = place()
    last = nz * nf - 1
    rows = x.shape[0]
    chunks = raw.shape[0]
    gw = chunks * WIDTH
    di = gw * GROUPS
    heads = dt.shape[1]
    own = taps_in.shape[1]

    def peer(d):
        return {"fsdp": f, "ctx": z * GROUPS + lax.rem(g + d, GROUPS)}

    def sibling(d):
        return {"fsdp": lax.rem(f + d, nf), "ctx": c}

    def along(half, k):
        return {"fsdp": half, "ctx": k * GROUPS + g}

    def tail_copy():
        return pltpu.make_async_copy(x.at[pl.ds(rows - HALO, HALO), :], tail, own_sem.at[1])

    sends_halo = jnp.logical_and(g == GROUPS - 1, seg < last)
    sends_half = jnp.logical_and(z == nz - 1, f < nf - 1)
    tells_plane = jnp.logical_and(g == GROUPS - 1, z < nz - 1)

    barrier = pltpu.get_barrier_semaphore()
    for d in range(1, GROUPS):
        pl.semaphore_signal(barrier, inc=1, device_id=peer(d))
    for d in range(1, nf):
        pl.semaphore_signal(barrier, inc=1, device_id=sibling(d))

    @pl.when(z < nz - 1)
    def _():
        pl.semaphore_signal(barrier, inc=1, device_id=along(f, z + 1))

    @pl.when(tells_plane)
    def _():
        for p in range(GROUPS):
            pl.semaphore_signal(barrier, inc=1, device_id=device(seg + 1, p, nz))

    @pl.when(f > 0)
    def _():
        pl.semaphore_signal(barrier, inc=1, device_id=along(f - 1, nz - 1))

    @pl.when(jnp.logical_and(f > 0, z == 0))
    def _():
        pl.semaphore_signal(barrier, inc=1, device_id=device(seg - 1, GROUPS - 1, nz))

    steps_in = pltpu.make_async_copy(dt, dt_own, own_sem.at[0])
    steps_in.start()

    @pl.when(sends_halo)
    def _():
        tail_copy().start()

    more = jnp.where(z > 0, 2, 0) + jnp.where(sends_half, jnp.where(g == GROUPS - 1, nz + GROUPS, nz), 0)
    pl.semaphore_wait(barrier, GROUPS - 1 + nf - 1 + more)

    def b_at(p):
        return pl.ds(pl.multiple_of(di + p * N, 128), N)

    def c_at(p):
        return pl.ds(pl.multiple_of(di + (GROUPS + p) * N, 128), N)

    mine = pl.ds(pl.multiple_of(g * rows, 128), rows)

    def halo_copies():
        return [pltpu.make_async_remote_copy(
            packs.at[p], halo, tsend.at[0], trecv.at[0], device_id=device(seg + 1, p, nz))
            for p in range(GROUPS)]

    params = [(taps_in, taps.at[:, lanes(f, own)]), (bias_in, biases.at[f]), (step_in, vectors.at[0, f]),
              (rate_in, vectors.at[1, f]), (skip_in, vectors.at[2, f]), (gain_in, gain_ref.at[f])]

    def states(p):
        return [(x.at[:, b_at(p)], raw_bc.at[mine, 0:N]), (x.at[:, c_at(p)], raw_bc.at[mine, N : 2 * N])]

    def pieces(q):
        out = []
        for d in (2, 1, 3):
            p = lax.rem(g + d, GROUPS)
            out.append(pltpu.make_async_remote_copy(
                x.at[:, lanes(p * chunks + q, WIDTH)], raw.at[q, mine], xsend.at[0],
                xrecv.at[q], device_id=peer(d)))
        out.append(pltpu.make_async_copy(
            x.at[:, lanes(g * chunks + q, WIDTH)], raw.at[q, mine], xrecv.at[q]))
        return out

    slots = (0, 1, 2, 2, 2, 3)
    state_copies, step_copies, param_copies, local_copies = [], [], [], []
    for d in (2, 1, 3):
        p = lax.rem(g + d, GROUPS)
        for k, (src, dst) in enumerate(states(p)):
            state_copies.append(pltpu.make_async_remote_copy(
                src, dst, bsend.at[0], brecv.at[0], device_id=peer(d)))
        step_copies.append(pltpu.make_async_remote_copy(
            dt_packs.at[p], dts.at[g], bsend.at[1], brecv.at[1], device_id=peer(d)))
    for d in range(1, nf):
        for k, (src, dst) in enumerate(params):
            param_copies.append(pltpu.make_async_remote_copy(
                src, dst, psend.at[slots[k]], precv.at[slots[k]], device_id=sibling(d)))
    for src, dst in states(g):
        local_copies.append(pltpu.make_async_copy(src, dst, brecv.at[0]))
    for k, (src, dst) in enumerate(params):
        local_copies.append(pltpu.make_async_copy(src, dst, precv.at[slots[k]]))

    early = min(2, chunks)
    for copy in state_copies:
        copy.start()
    for copy in pieces(0):
        copy.start()
    @pl.when(z > 0)
    def _():
        pl.semaphore_signal(chain_ready, inc=1, device_id=along(f, z - 1))
        pl.semaphore_signal(plane_ready, inc=1, device_id=device(seg - 1, GROUPS - 1, nz))

    for copy in param_copies + local_copies:
        copy.start()

    steps_in.wait()
    part = rows // GROUPS
    slot = lax.broadcasted_iota(jnp.int32, (part, heads), 1) // (heads // GROUPS)
    blocks = [dt_own[k * part : (k + 1) * part, :].astype(F32) for k in range(GROUPS)]
    for p in range(GROUPS):
        packed = jnp.zeros((part, heads), F32)
        for k in range(GROUPS):
            turned = pltpu.roll(blocks[k], (k - p) % GROUPS * (heads // GROUPS), 1)
            packed = jnp.where(slot == k, turned, packed)
        dt_packs[p] = packed.astype(BF16)
    for copy in step_copies:
        copy.start()
    dts[g] = dt_packs[g]

    for q in range(1, early):
        for copy in pieces(q):
            copy.start()

    @pl.when(sends_halo)
    def _():
        packing[...] = jnp.zeros_like(packing)
        tail_copy().wait()
        for p in range(GROUPS):
            starts = [p * gw + k * WIDTH for k in range(chunks)]
            for k, at in enumerate(starts):
                packing[3 * k : 3 * k + 3, :] = tail[:, at : at + WIDTH].astype(F32)[HALO - 3 :]
            for k, at in enumerate((di + p * N, di + (GROUPS + p) * N)):
                packing[3 * chunks : 3 * chunks + 3, k * N : (k + 1) * N] = (
                    tail[:, at : at + N].astype(F32)[HALO - 3 :])
            packs[p] = packing[...].astype(BF16)

        @pl.when(tells_plane)
        def _():
            pl.semaphore_wait(plane_ready, GROUPS)

        for copy in halo_copies():
            copy.start()

    @pl.loop(early, chunks)
    def _(q):
        for copy in pieces(q):
            copy.start()

    @pl.when(z == 0)
    def _():
        a_buf[...] = jnp.zeros_like(a_buf)

    @pl.when(f == 0)
    def _():
        h_buf[...] = jnp.zeros_like(h_buf)

    @pl.when(z == 0)
    def _():
        decays[...] = jnp.ones_like(decays)

    fill_selection(sel)
    squares[...] = jnp.zeros_like(squares)
    halos[...] = jnp.zeros_like(halos)
    take(raw_bc, brecv.at[0])
    take(dt_packs.at[0 : GROUPS - 1], brecv.at[1])
    take(taps, precv.at[0])
    take(biases, precv.at[1])
    take(vectors, precv.at[2])
    take(gain_ref, precv.at[3])

    @pl.when(seg > 0)
    def _():
        halo_copies()[0].wait_recv()
        for k in range(chunks + 1):
            halos[k, 5:8, :] = halo[...].astype(F32)[3 * k : 3 * k + 3]

    per_bias = own // 128

    def bias_of(i):
        return biases[i // per_bias, pl.ds(lax.rem(i, per_bias), 1), :]

    ext[0:8, :] = halos[chunks]
    ext[8:, :] = raw_bc[...].astype(F32)
    keys[...] = silu_conv(ext, 0, taps, bias_of(di // N + g), b_at(g), N)
    queries = silu_conv(ext, N, taps, bias_of(di // N + GROUPS + g), c_at(g), N)
    to_front = lax.rem(GROUPS - g, GROUPS) * (heads // GROUPS)
    step_bias, rate_log, direct = (
        pltpu.roll(jnp.broadcast_to(jnp.concatenate([vectors[k, i] for i in range(nf)], axis=1), (8, heads)),
                   to_front, 1)[0:1] for k in range(3))
    lower = (lax.broadcasted_iota(jnp.int32, (rows, rows), 0)
             >= lax.broadcasted_iota(jnp.int32, (rows, rows), 1))
    ones = jnp.where(lower, 1.0, 0.0)
    scale = jnp.exp(rate_log)
    decayed = jnp.ones((1, heads), F32)
    for j in range(GROUPS):
        at = pl.ds(j * rows, rows)
        steps_of = dts[j].astype(F32)
        delta = jnp.concatenate(
            [pltpu.roll(steps_of, (GROUPS - k) % GROUPS * (heads // GROUPS), 1) for k in range(GROUPS)],
            axis=0) + step_bias
        delta = jnp.maximum(delta, 0.0) + jnp.log1p(jnp.exp(-jnp.abs(delta)))
        cum = lax.dot_general(ones, -scale * delta, (((1,), (0,)), ((), ())),
                              precision=lax.Precision.HIGHEST, preferred_element_type=F32)
        decay = jnp.exp(cum)
        source[j] = hi_lo(delta * jnp.exp(-cum))
        decay_2[j] = hi_lo(decay)
        carry_2[j] = hi_lo(decay * decayed)
        block_decay = decay[rows - 1 : rows, :]
        decayed = decayed * block_decay
        vec_2[j] = hi_lo(jnp.concatenate(
            [direct, block_decay, decayed, jnp.zeros((5, heads), F32)], axis=0))
        mine_q = queries[j * rows : (j + 1) * rows]
        scores = jnp.where(lower, dot(mine_q, keys[at, :], ((1,), (1,))), 0.0).astype(BF16)
        left[j] = jnp.concatenate([scores, mine_q], axis=1)
    my_decay[...] = jnp.broadcast_to(decayed, (8, heads))

    def decay_hop():
        return pltpu.make_async_remote_copy(
            next_decay, decays, dsend.at[0], drecv.at[0], device_id=along(f, z + 1))

    def local_step(q):
        take(raw.at[q], xrecv.at[q])
        here = lanes(q, WIDTH)
        ext[0:8, :] = halos[q]
        ext[8:, :] = raw[q].astype(F32)
        i = g * chunks + q
        bias = jnp.concatenate([bias_of(2 * i), bias_of(2 * i + 1)], axis=1)
        act = silu_conv(ext, 0, taps, bias, lanes(i, WIDTH), WIDTH)
        pick = sel[:, here]
        state = jnp.zeros((N, WIDTH), F32)
        for j in range(GROUPS):
            values = act[j * rows : (j + 1) * rows].astype(F32)
            weighted = (values * dot(source[j], pick)).astype(BF16)
            vec = dot(vec_2[j], pick)
            inner = dot(left[j], jnp.concatenate([weighted, state.astype(BF16)], axis=0))
            z_buf[q, j] = dot(decay_2[j], pick) * inner + vec[0:1, :] * values
            state = vec[1:2, :] * (state + dot(keys[pl.ds(j * rows, rows), :], weighted, ((0,), (0,))))
        p_buf[q] = state

    def hop(q):
        return pltpu.make_async_remote_copy(
            a_out.at[q], a_buf.at[q], csend.at[0], crecv.at[q], device_id=along(f, z + 1))

    def half(q, k):
        return pltpu.make_async_remote_copy(
            h_out.at[q], h_buf.at[q], hsend.at[k], hrecv.at[q], device_id=along(f + 1, k))

    def back(d, first, size):
        here = pl.ds(pl.multiple_of(first * WIDTH, 128), size * WIDTH)
        there = pl.ds(pl.multiple_of(g * gw + first * WIDTH, 128), size * WIDTH)
        return pltpu.make_async_remote_copy(
            y_out.at[lax.rem(g + d, GROUPS), :, here], y_ref.at[:, there],
            osend.at[0], orecv.at[jnp.maximum(first - chunks + LATE + 1, 0)], device_id=peer(d))

    def through(pick):
        return dot(vec_2[GROUPS - 1], pick)[2:3, :]

    def chain_step(q):
        @pl.when(z > 0)
        def _():
            hop(q).wait_recv()

        @pl.when(z < nz - 1)
        def _():
            pick = sel[:, lanes(q, WIDTH)]
            a_out[q] = (p_buf[q] + through(pick) * a_buf[q].astype(F32)).astype(a_out.dtype)
            hop(q).start()

    def carry_step(q):
        pick = sel[:, lanes(q, WIDTH)]

        @pl.when(f > 0)
        def _():
            half(q, 0).wait_recv()

        state = a_buf[q].astype(F32) + dot(before_2[...], pick)[0:1, :] * h_buf[q].astype(F32)

        @pl.when(sends_half)
        def _():
            h_out[q] = (p_buf[q] + through(pick) * state).astype(h_out.dtype)
            for k in range(nz):
                half(q, k).start()

        low = state.astype(BF16)
        for j in range(GROUPS):
            carried = dot(left[j, :, N:], low) * dot(carry_2[j], pick)
            y_out[j, :, lanes(q, WIDTH)] = (z_buf[q, j] + carried).astype(BF16)

        @pl.when(q >= chunks - LATE)
        def _():
            for d in range(1, GROUPS):
                back(d, q, 1).start()

        @pl.when(jnp.logical_and(q < chunks - LATE, lax.rem(q, 2) == 1))
        def _():
            for d in range(1, GROUPS):
                back(d, q - 1, 2).start()

        y_ref[:, lanes(g * chunks + q, WIDTH)] = y_out[g, :, lanes(q, WIDTH)]

    def bounded(v):
        return jnp.where(v < chunks, v, chunks)

    chain_lag = bounded(z)
    carry_lag = bounded(jnp.where(f == 0, z, nz - 1 + f))
    steps = chunks + min(chunks, nz - 1 + nf - 1)

    @pl.loop(0, steps)
    def _(i):
        @pl.when(i < chunks)
        def _():
            local_step(i)

        @pl.when(i == chain_lag)
        def _():
            @pl.when(z > 0)
            def _():
                decay_hop().wait_recv()

            before_2[...] = hi_lo(decays[...])

            @pl.when(z < nz - 1)
            def _():
                pl.semaphore_wait(chain_ready, 1)
                next_decay[...] = decays[...] * my_decay[...]
                decay_hop().start()

        @pl.when(jnp.logical_and(i >= chain_lag, i < chain_lag + chunks))
        def _():
            chain_step(i - chain_lag)

        @pl.when(jnp.logical_and(i >= carry_lag, i < carry_lag + chunks))
        def _():
            carry_step(i - carry_lag)

    others = (GROUPS - 1) * rows
    take(raw.at[:, 0:others], xsend.at[0])
    take(raw_bc.at[0:others], bsend.at[0])
    take(dt_packs.at[0 : GROUPS - 1], bsend.at[1])
    take(taps.at[:, 0 : (nf - 1) * own], psend.at[0])
    take(biases.at[0 : nf - 1], psend.at[1])
    take(vectors.at[:, 0 : nf - 1], psend.at[2])
    take(gain_ref.at[0 : nf - 1], psend.at[3])

    @pl.when(z < nz - 1)
    def _():
        decay_hop().wait_send()

        take(a_out, csend.at[0])

    @pl.when(sends_half)
    def _():
        for k in range(nz):
            take(h_out, hsend.at[k])

    @pl.when(sends_halo)
    def _():
        take(packs, tsend.at[0])

    def add_squares(q):
        for p in range(GROUPS):
            y = y_ref[:, lanes(p * chunks + q, WIDTH)].astype(F32)
            squares[p] = squares[p] + y * y

    take(y_out.at[0 : GROUPS - 1, :, 0 : (chunks - LATE) * WIDTH], orecv.at[0])
    pl.loop(0, chunks - LATE)(add_squares)

    @pl.loop(chunks - LATE, chunks)
    def _(q):
        take(y_out.at[0 : GROUPS - 1, :, lanes(q, WIDTH)], orecv.at[q - chunks + LATE + 1])
        add_squares(q)

    take(y_out.at[0 : GROUPS - 1], osend.at[0])

    for p in range(GROUPS):
        norm = lax.rsqrt(jnp.sum(squares[p], axis=1, keepdims=True) * (1.0 / gw) + 1e-05)
        scale_ref[:, p * 128 : (p + 1) * 128] = jnp.broadcast_to(norm, (rows, 128))


def mixer(x, dt, taps, bias, step, rate, skip, gain):
    rows, ch = x.shape
    heads = dt.shape[1]
    nf = lax.axis_size("fsdp")
    nz = lax.axis_size("ctx") // GROUPS
    gw = heads * P_SIZE // GROUPS
    chunks = gw // WIDTH
    length = rows * GROUPS
    packed_rows = -(-3 * (chunks + 1) // 16) * 16
    link = BF16 if nf * nz <= 8 else F32
    vm, dma = pltpu.VMEM, pltpu.SemaphoreType.DMA
    return pl.pallas_call(
        mixer_kernel,
        out_shape=(jax.ShapeDtypeStruct((rows, gw * GROUPS), BF16),
                   jax.ShapeDtypeStruct((rows, GROUPS * 128), F32),
                   jax.ShapeDtypeStruct((nf,) + gain.shape, F32)),
        in_specs=[HBM] * 8,
        out_specs=(WHOLE,) * 3,
        scratch_shapes=[
            vm((chunks, length, WIDTH), BF16),
            vm((length, 2 * N), BF16),
            vm((rows, heads), BF16),
            vm((GROUPS, rows // GROUPS, heads), BF16),
            vm((GROUPS, rows // GROUPS, heads), BF16),
            vm((HALO, ch), BF16),
            vm((packed_rows, WIDTH), F32),
            vm((GROUPS, packed_rows, WIDTH), BF16),
            vm((packed_rows, WIDTH), BF16),
            vm((chunks + 1, 8, WIDTH), F32),
            vm((4, ch), F32),
            vm((nf,) + bias.shape, F32),
            vm((3, nf) + step.shape, F32),
            vm((2 * heads, gw), BF16),
            vm((8 + length, WIDTH), F32),
            vm((length, N), BF16),
            vm((GROUPS, rows, 2 * N), BF16),
            vm((GROUPS, rows, 2 * heads), BF16),
            vm((GROUPS, rows, 2 * heads), BF16),
            vm((GROUPS, rows, 2 * heads), BF16),
            vm((GROUPS, 8, 2 * heads), BF16),
            vm((8, heads), F32),
            vm((8, heads), F32),
            vm((8, heads), F32),
            vm((8, 2 * heads), BF16),
            vm((chunks, GROUPS, rows, WIDTH), F32),
            vm((chunks, N, WIDTH), F32),
            vm((chunks, N, WIDTH), link),
            vm((chunks, N, WIDTH), link),
            vm((chunks, N, WIDTH), link),
            vm((chunks, N, WIDTH), link),
            vm((GROUPS, rows, gw), BF16),
            vm((GROUPS, rows, WIDTH), F32),
            dma((1,)), dma((chunks,)), dma((2,)), dma((2,)), dma((4,)), dma((4,)), dma((1,)), dma((1,)),
            dma((1,)), dma((1,)), dma((1,)), dma((chunks,)), dma((nz,)), dma((chunks,)),
            dma((1,)), dma((LATE + 1,)), dma((2,)), pltpu.SemaphoreType.REGULAR, pltpu.SemaphoreType.REGULAR,
        ],
        compiler_params=pltpu.CompilerParams(
            collective_id=0, has_side_effects=True, vmem_limit_bytes=51 << 20),
        name="mixer",
    )(x, dt, taps, bias, step, rate, skip, gain)


def norm_kernel(y, scale, gain, out, buf, sem):
    gw = y.shape[1] // GROUPS
    own = gain.shape[2]
    part = gw // 4
    copies = []
    for p in range(GROUPS):
        for k in range(4):
            for at in range(p * gw + k * part, p * gw + (k + 1) * part, 128):
                gains = gain[at // own, :, at % own : at % own + 128]
                buf[:, at : at + 128] = (
                    y[:, at : at + 128].astype(F32) * scale[:, p * 128 : (p + 1) * 128] * gains).astype(BF16)
            here = slice(p * gw + k * part, p * gw + (k + 1) * part)
            copies.append(pltpu.make_async_copy(buf.at[:, here], out.at[:, here], sem.at[p * 4 + k]))
            copies[-1].start()
    for copy in copies:
        copy.wait()


def norm(y, scale, gain):
    return pl.pallas_call(
        norm_kernel,
        out_shape=jax.ShapeDtypeStruct(y.shape, BF16),
        in_specs=[WHOLE] * 3,
        out_specs=HBM,
        scratch_shapes=[pltpu.VMEM(y.shape, BF16), pltpu.SemaphoreType.DMA((16,))],
        compiler_params=pltpu.CompilerParams(vmem_limit_bytes=16 << 20),
        name="norm",
    )(y, scale, gain)


def local(xbc, dt, conv_weight, conv_bias, dt_bias, a_log, skip, norm_gain):
    y, scale, gain = mixer(*(pltpu.with_memory_space_constraint(v, pltpu.HBM) for v in (
        xbc, dt, conv_weight, conv_bias.reshape(-1, 128), dt_bias.reshape(1, -1), a_log.reshape(1, -1),
        skip.reshape(1, -1), norm_gain.reshape(1, -1))))
    return norm(y, scale, gain)


def solution(mesh):
    placed = (
        P(("fsdp", "ctx"), None),
        P(("fsdp", "ctx"), None),
        P(None, "fsdp"),
        P("fsdp"),
        P("fsdp"),
        P("fsdp"),
        P("fsdp"),
        P("fsdp"),
    )
    return jax.shard_map(
        local, mesh=mesh, in_specs=placed, out_specs=P(("fsdp", "ctx"), None), check_vma=False
    )
```

```python
import jax
import jax.numpy as jnp
from jax import lax
from jax.experimental import pallas as pl
from jax.experimental.pallas import tpu as pltpu
from jax.sharding import PartitionSpec as P

P_SIZE = 64
N = 128
GROUPS = 4
HALO = 16
WIDTH = 256
LATE = 2
F32, BF16 = jnp.float32, jnp.bfloat16
HBM = pl.BlockSpec(memory_space=pltpu.HBM)
WHOLE = pl.BlockSpec(memory_space=pltpu.VMEM)


def place():
    f, c = lax.axis_index("fsdp"), lax.axis_index("ctx")
    nz = lax.axis_size("ctx") // GROUPS
    nf = lax.axis_size("fsdp")
    g, z = lax.rem(c, GROUPS), c // GROUPS
    return f, c, g, z, nz, nf, f * nz + z


def device(seg, g, nz):
    return {"fsdp": seg // nz, "ctx": lax.rem(seg, nz) * GROUPS + g}


def lanes(index, size):
    return pl.ds(pl.multiple_of(index * size, 128), size)


def hi_lo(v):
    hi = v.astype(BF16)
    return jnp.concatenate([hi, (v - hi.astype(F32)).astype(BF16)], axis=1)


def dot(a, b, dims=((1,), (0,))):
    return lax.dot_general(a, b, (dims, ((), ())), preferred_element_type=F32)


def fill_selection(sel):
    heads = sel.shape[0] // 2
    row = lax.broadcasted_iota(jnp.int32, sel.shape, 0)
    col = lax.broadcasted_iota(jnp.int32, sel.shape, 1)
    row = jnp.where(row >= heads, row - heads, row)
    sel[...] = jnp.where(row == col // P_SIZE, 1.0, 0.0).astype(BF16)


def take(ref, sem):
    pltpu.make_async_copy(ref, ref, sem).wait()


def silu_conv(ext, start, taps, bias, at, size):
    rows = ext.shape[0] - 8
    total = bias
    for k in range(4):
        total = total + taps[k : k + 1, at] * ext[5 + k : 5 + k + rows, start : start + size]
    return (total / (1.0 + jnp.exp(-total))).astype(BF16)


def mixer_kernel(x, dt, taps_in, bias_in, step_in, rate_in, skip_in, gain_in,
                 y_ref, scale_ref, gain_ref,
                 raw, raw_bc, dt_own, dt_packs, dts, tail, packing, packs, halo, halos, taps, biases, vectors, sel, ext, keys, left, source, decay_2,
                 carry_2, vec_2, my_decay, next_decay, decays, before_2, z_buf, p_buf, a_buf, a_out, h_buf, h_out,
                 y_out, squares,
                 xsend, xrecv, bsend, brecv, psend, precv, tsend, trecv, dsend, drecv, csend, crecv,
                 hsend, hrecv, osend, orecv, own_sem, chain_ready, plane_ready):
    f, c, g, z, nz, nf, seg = place()
    last = nz * nf - 1
    rows = x.shape[0]
    chunks = raw.shape[0]
    gw = chunks * WIDTH
    di = gw * GROUPS
    heads = dt.shape[1]
    own = taps_in.shape[1]

    def peer(d):
        return {"fsdp": f, "ctx": z * GROUPS + lax.rem(g + d, GROUPS)}

    def sibling(d):
        return {"fsdp": lax.rem(f + d, nf), "ctx": c}

    def along(half, k):
        return {"fsdp": half, "ctx": k * GROUPS + g}

    def tail_copy():
        return pltpu.make_async_copy(x.at[pl.ds(rows - HALO, HALO), :], tail, own_sem.at[1])

    sends_halo = jnp.logical_and(g == GROUPS - 1, seg < last)
    sends_half = jnp.logical_and(z == nz - 1, f < nf - 1)
    tells_plane = jnp.logical_and(g == GROUPS - 1, z < nz - 1)

    barrier = pltpu.get_barrier_semaphore()
    for d in range(1, GROUPS):
        pl.semaphore_signal(barrier, inc=1, device_id=peer(d))
    for d in range(1, nf):
        pl.semaphore_signal(barrier, inc=1, device_id=sibling(d))

    @pl.when(z < nz - 1)
    def _():
        pl.semaphore_signal(barrier, inc=1, device_id=along(f, z + 1))

    @pl.when(tells_plane)
    def _():
        for p in range(GROUPS):
            pl.semaphore_signal(barrier, inc=1, device_id=device(seg + 1, p, nz))

    @pl.when(f > 0)
    def _():
        pl.semaphore_signal(barrier, inc=1, device_id=along(f - 1, nz - 1))

    @pl.when(jnp.logical_and(f > 0, z == 0))
    def _():
        pl.semaphore_signal(barrier, inc=1, device_id=device(seg - 1, GROUPS - 1, nz))

    steps_in = pltpu.make_async_copy(dt, dt_own, own_sem.at[0])
    steps_in.start()

    @pl.when(sends_halo)
    def _():
        tail_copy().start()

    more = jnp.where(z > 0, 2, 0) + jnp.where(sends_half, jnp.where(g == GROUPS - 1, nz + GROUPS, nz), 0)
    pl.semaphore_wait(barrier, GROUPS - 1 + nf - 1 + more)

    def b_at(p):
        return pl.ds(pl.multiple_of(di + p * N, 128), N)

    def c_at(p):
        return pl.ds(pl.multiple_of(di + (GROUPS + p) * N, 128), N)

    mine = pl.ds(pl.multiple_of(g * rows, 128), rows)

    def halo_copies():
        return [pltpu.make_async_remote_copy(
            packs.at[p], halo, tsend.at[0], trecv.at[0], device_id=device(seg + 1, p, nz))
            for p in range(GROUPS)]

    params = [(taps_in, taps.at[:, lanes(f, own)]), (bias_in, biases.at[f]), (step_in, vectors.at[0, f]),
              (rate_in, vectors.at[1, f]), (skip_in, vectors.at[2, f]), (gain_in, gain_ref.at[f])]

    def states(p):
        return [(x.at[:, b_at(p)], raw_bc.at[mine, 0:N]), (x.at[:, c_at(p)], raw_bc.at[mine, N : 2 * N])]

    def pieces(q):
        out = []
        for d in (2, 1, 3):
            p = lax.rem(g + d, GROUPS)
            out.append(pltpu.make_async_remote_copy(
                x.at[:, lanes(p * chunks + q, WIDTH)], raw.at[q, mine], xsend.at[0],
                xrecv.at[q], device_id=peer(d)))
        out.append(pltpu.make_async_copy(
            x.at[:, lanes(g * chunks + q, WIDTH)], raw.at[q, mine], xrecv.at[q]))
        return out

    slots = (0, 1, 2, 2, 2, 3)
    state_copies, step_copies, param_copies, local_copies = [], [], [], []
    for d in (2, 1, 3):
        p = lax.rem(g + d, GROUPS)
        for k, (src, dst) in enumerate(states(p)):
            state_copies.append(pltpu.make_async_remote_copy(
                src, dst, bsend.at[0], brecv.at[0], device_id=peer(d)))
        step_copies.append(pltpu.make_async_remote_copy(
            dt_packs.at[p], dts.at[g], bsend.at[1], brecv.at[1], device_id=peer(d)))
    for d in range(1, nf):
        for k, (src, dst) in enumerate(params):
            param_copies.append(pltpu.make_async_remote_copy(
                src, dst, psend.at[slots[k]], precv.at[slots[k]], device_id=sibling(d)))
    for src, dst in states(g):
        local_copies.append(pltpu.make_async_copy(src, dst, brecv.at[0]))
    for k, (src, dst) in enumerate(params):
        local_copies.append(pltpu.make_async_copy(src, dst, precv.at[slots[k]]))

    early = min(2, chunks)
    for copy in state_copies:
        copy.start()
    for copy in pieces(0):
        copy.start()
    @pl.when(z > 0)
    def _():
        pl.semaphore_signal(chain_ready, inc=1, device_id=along(f, z - 1))
        pl.semaphore_signal(plane_ready, inc=1, device_id=device(seg - 1, GROUPS - 1, nz))

    for copy in param_copies + local_copies:
        copy.start()

    steps_in.wait()
    part = rows // GROUPS
    slot = lax.broadcasted_iota(jnp.int32, (part, heads), 1) // (heads // GROUPS)
    blocks = [dt_own[k * part : (k + 1) * part, :].astype(F32) for k in range(GROUPS)]
    for p in range(GROUPS):
        packed = jnp.zeros((part, heads), F32)
        for k in range(GROUPS):
            turned = pltpu.roll(blocks[k], (k - p) % GROUPS * (heads // GROUPS), 1)
            packed = jnp.where(slot == k, turned, packed)
        dt_packs[p] = packed.astype(BF16)
    for copy in step_copies:
        copy.start()
    dts[g] = dt_packs[g]

    for q in range(1, early):
        for copy in pieces(q):
            copy.start()

    @pl.when(sends_halo)
    def _():
        packing[...] = jnp.zeros_like(packing)
        tail_copy().wait()
        for p in range(GROUPS):
            starts = [p * gw + k * WIDTH for k in range(chunks)]
            for k, at in enumerate(starts):
                packing[3 * k : 3 * k + 3, :] = tail[:, at : at + WIDTH].astype(F32)[HALO - 3 :]
            for k, at in enumerate((di + p * N, di + (GROUPS + p) * N)):
                packing[3 * chunks : 3 * chunks + 3, k * N : (k + 1) * N] = (
                    tail[:, at : at + N].astype(F32)[HALO - 3 :])
            packs[p] = packing[...].astype(BF16)

        @pl.when(tells_plane)
        def _():
            pl.semaphore_wait(plane_ready, GROUPS)

        for copy in halo_copies():
            copy.start()

    @pl.loop(early, chunks)
    def _(q):
        for copy in pieces(q):
            copy.start()

    @pl.when(z == 0)
    def _():
        a_buf[...] = jnp.zeros_like(a_buf)

    @pl.when(f == 0)
    def _():
        h_buf[...] = jnp.zeros_like(h_buf)

    @pl.when(z == 0)
    def _():
        decays[...] = jnp.ones_like(decays)

    fill_selection(sel)
    squares[...] = jnp.zeros_like(squares)
    halos[...] = jnp.zeros_like(halos)
    take(raw_bc, brecv.at[0])
    take(dt_packs.at[0 : GROUPS - 1], brecv.at[1])
    take(taps, precv.at[0])
    take(biases, precv.at[1])
    take(vectors, precv.at[2])
    take(gain_ref, precv.at[3])

    @pl.when(seg > 0)
    def _():
        halo_copies()[0].wait_recv()
        for k in range(chunks + 1):
            halos[k, 5:8, :] = halo[...].astype(F32)[3 * k : 3 * k + 3]

    per_bias = own // 128

    def bias_of(i):
        return biases[i // per_bias, pl.ds(lax.rem(i, per_bias), 1), :]

    ext[0:8, :] = halos[chunks]
    ext[8:, :] = raw_bc[...].astype(F32)
    keys[...] = silu_conv(ext, 0, taps, bias_of(di // N + g), b_at(g), N)
    queries = silu_conv(ext, N, taps, bias_of(di // N + GROUPS + g), c_at(g), N)
    to_front = lax.rem(GROUPS - g, GROUPS) * (heads // GROUPS)
    step_bias, rate_log, direct = (
        pltpu.roll(jnp.broadcast_to(jnp.concatenate([vectors[k, i] for i in range(nf)], axis=1), (8, heads)),
                   to_front, 1)[0:1] for k in range(3))
    lower = (lax.broadcasted_iota(jnp.int32, (rows, rows), 0)
             >= lax.broadcasted_iota(jnp.int32, (rows, rows), 1))
    ones = jnp.where(lower, 1.0, 0.0)
    scale = jnp.exp(rate_log)
    decayed = jnp.ones((1, heads), F32)
    for j in range(GROUPS):
        at = pl.ds(j * rows, rows)
        steps_of = dts[j].astype(F32)
        delta = jnp.concatenate(
            [pltpu.roll(steps_of, (GROUPS - k) % GROUPS * (heads // GROUPS), 1) for k in range(GROUPS)],
            axis=0) + step_bias
        delta = jnp.maximum(delta, 0.0) + jnp.log1p(jnp.exp(-jnp.abs(delta)))
        cum = lax.dot_general(ones, -scale * delta, (((1,), (0,)), ((), ())),
                              precision=lax.Precision.HIGHEST, preferred_element_type=F32)
        decay = jnp.exp(cum)
        source[j] = hi_lo(delta * jnp.exp(-cum))
        decay_2[j] = hi_lo(decay)
        carry_2[j] = hi_lo(decay * decayed)
        block_decay = decay[rows - 1 : rows, :]
        decayed = decayed * block_decay
        vec_2[j] = hi_lo(jnp.concatenate(
            [direct, block_decay, decayed, jnp.zeros((5, heads), F32)], axis=0))
        mine_q = queries[j * rows : (j + 1) * rows]
        scores = jnp.where(lower, dot(mine_q, keys[at, :], ((1,), (1,))), 0.0).astype(BF16)
        left[j] = jnp.concatenate([scores, mine_q], axis=1)
    my_decay[...] = jnp.broadcast_to(decayed, (8, heads))

    def decay_hop():
        return pltpu.make_async_remote_copy(
            next_decay, decays, dsend.at[0], drecv.at[0], device_id=along(f, z + 1))

    def local_step(q):
        take(raw.at[q], xrecv.at[q])
        here = lanes(q, WIDTH)
        ext[0:8, :] = halos[q]
        ext[8:, :] = raw[q].astype(F32)
        i = g * chunks + q
        bias = jnp.concatenate([bias_of(2 * i), bias_of(2 * i + 1)], axis=1)
        act = silu_conv(ext, 0, taps, bias, lanes(i, WIDTH), WIDTH)
        pick = sel[:, here]
        state = jnp.zeros((N, WIDTH), F32)
        for j in range(GROUPS):
            values = act[j * rows : (j + 1) * rows].astype(F32)
            weighted = (values * dot(source[j], pick)).astype(BF16)
            vec = dot(vec_2[j], pick)
            inner = dot(left[j], jnp.concatenate([weighted, state.astype(BF16)], axis=0))
            z_buf[q, j] = dot(decay_2[j], pick) * inner + vec[0:1, :] * values
            state = vec[1:2, :] * (state + dot(keys[pl.ds(j * rows, rows), :], weighted, ((0,), (0,))))
        p_buf[q] = state

    def hop(q):
        return pltpu.make_async_remote_copy(
            a_out.at[q], a_buf.at[q], csend.at[0], crecv.at[q], device_id=along(f, z + 1))

    def half(q, k):
        return pltpu.make_async_remote_copy(
            h_out.at[q], h_buf.at[q], hsend.at[k], hrecv.at[q], device_id=along(f + 1, k))

    def back(d, first, size):
        here = pl.ds(pl.multiple_of(first * WIDTH, 128), size * WIDTH)
        there = pl.ds(pl.multiple_of(g * gw + first * WIDTH, 128), size * WIDTH)
        return pltpu.make_async_remote_copy(
            y_out.at[lax.rem(g + d, GROUPS), :, here], y_ref.at[:, there],
            osend.at[0], orecv.at[jnp.maximum(first - chunks + LATE + 1, 0)], device_id=peer(d))

    def through(pick):
        return dot(vec_2[GROUPS - 1], pick)[2:3, :]

    def chain_step(q):
        @pl.when(z > 0)
        def _():
            hop(q).wait_recv()

        @pl.when(z < nz - 1)
        def _():
            pick = sel[:, lanes(q, WIDTH)]
            a_out[q] = (p_buf[q] + through(pick) * a_buf[q].astype(F32)).astype(a_out.dtype)
            hop(q).start()

    def carry_step(q):
        pick = sel[:, lanes(q, WIDTH)]

        @pl.when(f > 0)
        def _():
            half(q, 0).wait_recv()

        state = a_buf[q].astype(F32) + dot(before_2[...], pick)[0:1, :] * h_buf[q].astype(F32)

        @pl.when(sends_half)
        def _():
            h_out[q] = (p_buf[q] + through(pick) * state).astype(h_out.dtype)
            for k in range(nz):
                half(q, k).start()

        low = state.astype(BF16)
        for j in range(GROUPS):
            carried = dot(left[j, :, N:], low) * dot(carry_2[j], pick)
            y_out[j, :, lanes(q, WIDTH)] = (z_buf[q, j] + carried).astype(BF16)

        @pl.when(q >= chunks - LATE)
        def _():
            for d in range(1, GROUPS):
                back(d, q, 1).start()

        @pl.when(jnp.logical_and(q < chunks - LATE, lax.rem(q, 2) == 1))
        def _():
            for d in range(1, GROUPS):
                back(d, q - 1, 2).start()

        y_ref[:, lanes(g * chunks + q, WIDTH)] = y_out[g, :, lanes(q, WIDTH)]

    def bounded(v):
        return jnp.where(v < chunks, v, chunks)

    chain_lag = bounded(z)
    carry_lag = bounded(jnp.where(f == 0, jnp.maximum(z, 2), nz - 1 + f))
    steps = chunks + min(chunks, nz - 1 + nf - 1)

    @pl.loop(0, steps)
    def _(i):
        @pl.when(i < chunks)
        def _():
            local_step(i)

        @pl.when(i == chain_lag)
        def _():
            @pl.when(z > 0)
            def _():
                decay_hop().wait_recv()

            before_2[...] = hi_lo(decays[...])

            @pl.when(z < nz - 1)
            def _():
                pl.semaphore_wait(chain_ready, 1)
                next_decay[...] = decays[...] * my_decay[...]
                decay_hop().start()

        @pl.when(jnp.logical_and(i >= chain_lag, i < chain_lag + chunks))
        def _():
            chain_step(i - chain_lag)

        @pl.when(jnp.logical_and(i >= carry_lag, i < carry_lag + chunks))
        def _():
            carry_step(i - carry_lag)

    others = (GROUPS - 1) * rows
    take(raw.at[:, 0:others], xsend.at[0])
    take(raw_bc.at[0:others], bsend.at[0])
    take(dt_packs.at[0 : GROUPS - 1], bsend.at[1])
    take(taps.at[:, 0 : (nf - 1) * own], psend.at[0])
    take(biases.at[0 : nf - 1], psend.at[1])
    take(vectors.at[:, 0 : nf - 1], psend.at[2])
    take(gain_ref.at[0 : nf - 1], psend.at[3])

    @pl.when(z < nz - 1)
    def _():
        decay_hop().wait_send()

        take(a_out, csend.at[0])

    @pl.when(sends_half)
    def _():
        for k in range(nz):
            take(h_out, hsend.at[k])

    @pl.when(sends_halo)
    def _():
        take(packs, tsend.at[0])

    def add_squares(q):
        for p in range(GROUPS):
            y = y_ref[:, lanes(p * chunks + q, WIDTH)].astype(F32)
            squares[p] = squares[p] + y * y

    take(y_out.at[0 : GROUPS - 1, :, 0 : (chunks - LATE) * WIDTH], orecv.at[0])
    pl.loop(0, chunks - LATE)(add_squares)

    @pl.loop(chunks - LATE, chunks)
    def _(q):
        take(y_out.at[0 : GROUPS - 1, :, lanes(q, WIDTH)], orecv.at[q - chunks + LATE + 1])
        add_squares(q)

    take(y_out.at[0 : GROUPS - 1], osend.at[0])

    for p in range(GROUPS):
        norm = lax.rsqrt(jnp.sum(squares[p], axis=1, keepdims=True) * (1.0 / gw) + 1e-05)
        scale_ref[:, p * 128 : (p + 1) * 128] = jnp.broadcast_to(norm, (rows, 128))


def mixer(x, dt, taps, bias, step, rate, skip, gain):
    rows, ch = x.shape
    heads = dt.shape[1]
    nf = lax.axis_size("fsdp")
    nz = lax.axis_size("ctx") // GROUPS
    gw = heads * P_SIZE // GROUPS
    chunks = gw // WIDTH
    length = rows * GROUPS
    packed_rows = -(-3 * (chunks + 1) // 16) * 16
    link = BF16 if nf * nz <= 8 else F32
    vm, dma = pltpu.VMEM, pltpu.SemaphoreType.DMA
    return pl.pallas_call(
        mixer_kernel,
        out_shape=(jax.ShapeDtypeStruct((rows, gw * GROUPS), BF16),
                   jax.ShapeDtypeStruct((rows, GROUPS * 128), F32),
                   jax.ShapeDtypeStruct((nf,) + gain.shape, F32)),
        in_specs=[HBM] * 8,
        out_specs=(WHOLE,) * 3,
        scratch_shapes=[
            vm((chunks, length, WIDTH), BF16),
            vm((length, 2 * N), BF16),
            vm((rows, heads), BF16),
            vm((GROUPS, rows // GROUPS, heads), BF16),
            vm((GROUPS, rows // GROUPS, heads), BF16),
            vm((HALO, ch), BF16),
            vm((packed_rows, WIDTH), F32),
            vm((GROUPS, packed_rows, WIDTH), BF16),
            vm((packed_rows, WIDTH), BF16),
            vm((chunks + 1, 8, WIDTH), F32),
            vm((4, ch), F32),
            vm((nf,) + bias.shape, F32),
            vm((3, nf) + step.shape, F32),
            vm((2 * heads, gw), BF16),
            vm((8 + length, WIDTH), F32),
            vm((length, N), BF16),
            vm((GROUPS, rows, 2 * N), BF16),
            vm((GROUPS, rows, 2 * heads), BF16),
            vm((GROUPS, rows, 2 * heads), BF16),
            vm((GROUPS, rows, 2 * heads), BF16),
            vm((GROUPS, 8, 2 * heads), BF16),
            vm((8, heads), F32),
            vm((8, heads), F32),
            vm((8, heads), F32),
            vm((8, 2 * heads), BF16),
            vm((chunks, GROUPS, rows, WIDTH), F32),
            vm((chunks, N, WIDTH), F32),
            vm((chunks, N, WIDTH), link),
            vm((chunks, N, WIDTH), link),
            vm((chunks, N, WIDTH), link),
            vm((chunks, N, WIDTH), link),
            vm((GROUPS, rows, gw), BF16),
            vm((GROUPS, rows, WIDTH), F32),
            dma((1,)), dma((chunks,)), dma((2,)), dma((2,)), dma((4,)), dma((4,)), dma((1,)), dma((1,)),
            dma((1,)), dma((1,)), dma((1,)), dma((chunks,)), dma((nz,)), dma((chunks,)),
            dma((1,)), dma((LATE + 1,)), dma((2,)), pltpu.SemaphoreType.REGULAR, pltpu.SemaphoreType.REGULAR,
        ],
        compiler_params=pltpu.CompilerParams(
            collective_id=0, has_side_effects=True, vmem_limit_bytes=51 << 20),
        name="mixer",
    )(x, dt, taps, bias, step, rate, skip, gain)


def norm_kernel(y, scale, gain, out, buf, sem):
    gw = y.shape[1] // GROUPS
    own = gain.shape[2]
    part = gw // 4
    copies = []
    for p in range(GROUPS):
        for k in range(4):
            for at in range(p * gw + k * part, p * gw + (k + 1) * part, 128):
                gains = gain[at // own, :, at % own : at % own + 128]
                buf[:, at : at + 128] = (
                    y[:, at : at + 128].astype(F32) * scale[:, p * 128 : (p + 1) * 128] * gains).astype(BF16)
            here = slice(p * gw + k * part, p * gw + (k + 1) * part)
            copies.append(pltpu.make_async_copy(buf.at[:, here], out.at[:, here], sem.at[p * 4 + k]))
            copies[-1].start()
    for copy in copies:
        copy.wait()


def norm(y, scale, gain):
    return pl.pallas_call(
        norm_kernel,
        out_shape=jax.ShapeDtypeStruct(y.shape, BF16),
        in_specs=[WHOLE] * 3,
        out_specs=HBM,
        scratch_shapes=[pltpu.VMEM(y.shape, BF16), pltpu.SemaphoreType.DMA((16,))],
        compiler_params=pltpu.CompilerParams(vmem_limit_bytes=16 << 20),
        name="norm",
    )(y, scale, gain)


def local(xbc, dt, conv_weight, conv_bias, dt_bias, a_log, skip, norm_gain):
    y, scale, gain = mixer(*(pltpu.with_memory_space_constraint(v, pltpu.HBM) for v in (
        xbc, dt, conv_weight, conv_bias.reshape(-1, 128), dt_bias.reshape(1, -1), a_log.reshape(1, -1),
        skip.reshape(1, -1), norm_gain.reshape(1, -1))))
    return norm(y, scale, gain)


def solution(mesh):
    placed = (
        P(("fsdp", "ctx"), None),
        P(("fsdp", "ctx"), None),
        P(None, "fsdp"),
        P("fsdp"),
        P("fsdp"),
        P("fsdp"),
        P("fsdp"),
        P("fsdp"),
    )
    return jax.shard_map(
        local, mesh=mesh, in_specs=placed, out_specs=P(("fsdp", "ctx"), None), check_vma=False
    )
```
